32 devices in a mesh: groups: 2 (over y), inner: 8 (over z, x), outer: 2 (over core).
Axes of the slice: x: 2, y: 2, z: 4, core: 2. Of those that a mesh axis runs over, the one named last changes fastest.
Arguments:
- queries: bfloat16 [4096, 1024], P(('groups', 'outer', 'inner')), parts along dimension 0, may hold values from -6 to 6
- keys: bfloat16 [4096, 2, 1024], P(('groups', 'outer', 'inner')), parts along dimension 0, may hold values from -6 to 6
- values: bfloat16 [4096, 2, 1024], P(('groups', 'outer', 'inner')), parts along dimension 0, may hold values from -6 to 6
- log_gate: float32 [4096, 8], P(('groups', 'outer', 'inner')), parts along dimension 0, may hold values from -1 to 0, as said below
- out_gate: bfloat16 [4096, 1024], P(('groups', 'outer', 'inner')), parts along dimension 0, may hold values from -6 to 6
- norm_gain: float32 [128], replicated, may hold values from 0.1 to 1.9
Outputs:
- gated_output: bfloat16 [4096, 1024], P(('groups', 'outer', 'inner')), parts along dimension 0
The draws below stay inside these ranges and needn't reach their ends.
There are 2 independent parts, one for each index of `groups`. The reference program is written for one: setup_inputs(seed, part) draws one part's arguments, and reference() takes and returns one part's arrays. A program takes and returns all parts, laid end to end along the dimension named above; an argument that names none is the same for every part. Nothing has to cross between parts.
Inputs may be any that keep to these rules, and one draw needn't show every extreme that they name: `log_gate`: logarithm of the factor by which a head's state is scaled at a token; never positive.
All inputs are finite; a program needn't handle non-finite values.
Results may differ from the reference program's by a relative error of at most 0.001.
Values sent between devices are 32-bit elements; how exact they have to be, the bound alone decides.
A program may use at most 512 MiB of HBM per device.

```python
import jax
import jax.numpy as jnp
from jax import lax

HEAD_GROUP = 8
HEAD = 128
T_DEV = 128
TOKEN_TOTAL = 2048
WIDTH = 1024


def draw_log_gate(key, part):
    complete_keys = jax.random.split(key, 7)
    head_order = jax.random.permutation(complete_keys[0], HEAD_GROUP)
    slow_heads = head_order >= HEAD_GROUP // 2
    fast_rate = jnp.exp(jax.random.uniform(complete_keys[1], (HEAD_GROUP,), jnp.float32, jnp.log(1.0 / 50.0), jnp.log(1.0 / 30.0)))
    slow_rate = jnp.exp(jax.random.uniform(complete_keys[2], (HEAD_GROUP,), jnp.float32, jnp.log(0.05), jnp.log(0.25))) / TOKEN_TOTAL
    baseline_speed = jnp.where(slow_heads, slow_rate, fast_rate)
    random_wobble = jnp.exp(jax.random.uniform(complete_keys[3], (TOKEN_TOTAL, HEAD_GROUP), jnp.float32, jnp.log(0.5), jnp.log(2.0)))
    processor_multiplier = jnp.exp(jax.random.uniform(complete_keys[4], (TOKEN_TOTAL // T_DEV, HEAD_GROUP), jnp.float32, jnp.log(0.5), jnp.log(2.0)))
    processor_multiplier = jnp.repeat(processor_multiplier, T_DEV, axis=0)
    spike_positions = jax.random.randint(complete_keys[5], (2, HEAD_GROUP), 0, TOKEN_TOTAL)
    position_list = jnp.arange(TOKEN_TOTAL)[:, None]
    spike_mask = (position_list == spike_positions[0][None, :]) | (position_list == spike_positions[1][None, :])
    spike_slowdown = jnp.log(jax.random.uniform(complete_keys[6], (TOKEN_TOTAL, HEAD_GROUP), jnp.float32, 0.45, 0.8))
    return jnp.where(spike_mask, spike_slowdown, 0.0) - baseline_speed[None, :] * random_wobble * processor_multiplier


def level_of(stream_key, shape, cuts, smallest, top_value):
    level, own = 1.0, jax.random.fold_in(stream_key, 6)
    for position, shards_of in cuts:
        draws = jnp.exp(jax.random.uniform(jax.random.fold_in(own, position), (shards_of,), jnp.float32, smallest / len(cuts), top_value / len(cuts)))
        level = level * jnp.repeat(draws, shape[position] // shards_of).reshape([-1 if axis == position else 1 for axis in range(len(shape))])
    return level


def centred(rng, extent, spread, limit, shards=(), held_as=jnp.bfloat16):
    level = level_of(rng, extent, shards, -0.22, 0.18) if shards else 1.0
    values = jax.random.normal(rng, extent, jnp.float32) * spread * level
    return jnp.minimum(jnp.maximum(values, -limit), limit).astype(held_as)


def setup_inputs(seed: int = 0, part: int = 0) -> dict:
    splits = jax.random.split(jax.random.key(seed), 7)
    part_keys = jax.random.split(jax.random.fold_in(splits[6], part), 7)
    return {
        "queries": centred(part_keys[0], (TOKEN_TOTAL, WIDTH), 1.0, 6.0, ((0, 16),)),
        "keys": centred(part_keys[1], (TOKEN_TOTAL, 2, WIDTH), 1.0, 6.0, ((0, 16),)),
        "values": centred(part_keys[2], (TOKEN_TOTAL, 2, WIDTH), 1.0, 6.0, ((0, 16),)),
        "log_gate": draw_log_gate(jax.random.fold_in(jax.random.fold_in(splits[6], part), 71), part),
        "out_gate": centred(part_keys[4], (TOKEN_TOTAL, WIDTH), 1.0, 6.0, ((0, 16),)),
        "norm_gain": jnp.clip(1.0 + 0.18 * jax.random.normal(splits[5], (HEAD,), jnp.float32), 0.1, 1.9),
    }


highest = lax.Precision.HIGHEST
eps_norm = 1e-06

def reference(queries, keys, values, log_gate, out_gate, norm_gain):
    tok_count = queries.shape[0]
    query_rows = queries.astype(jnp.float32).reshape(tok_count, HEAD_GROUP, HEAD)
    raw_keys = keys.astype(jnp.float32).reshape(tok_count, 2, HEAD_GROUP, HEAD)
    unit_keys = raw_keys * lax.rsqrt(lax.optimization_barrier(jnp.sum(raw_keys * raw_keys, axis=-1, keepdims=True)) + eps_norm)
    value_rows = values.astype(jnp.float32).reshape(tok_count, 2, HEAD_GROUP, HEAD)
    decay_rows = jnp.exp(log_gate)

    def advance_token(carried_state, inputs):
        query_now, keys_now, values_now, decay_now = inputs
        carried_state = decay_now[:, None, None] * carried_state
        for reflection in range(2):
            unit_key = keys_now[reflection]
            projected = jnp.einsum('hd,hde->he', unit_key, carried_state, precision=highest)
            carried_state = carried_state + 2.0 * unit_key[:, :, None] * (values_now[reflection] - projected)[:, None, :]
        return (carried_state, jnp.einsum('hd,hde->he', query_now, carried_state, precision=highest))
    initial = jnp.zeros((HEAD_GROUP, HEAD, HEAD), jnp.float32)
    final_state, head_outputs = lax.scan(advance_token, initial, (query_rows, unit_keys, value_rows, decay_rows))
    scale_inv = lax.rsqrt(lax.optimization_barrier(jnp.mean(head_outputs * head_outputs, axis=-1, keepdims=True)) + eps_norm)
    gate_vals = jax.nn.silu(out_gate.astype(jnp.float32).reshape(tok_count, HEAD_GROUP, HEAD))
    result = head_outputs * scale_inv * norm_gain * gate_vals
    return result.reshape(tok_count, HEAD_GROUP * HEAD).astype(jnp.bfloat16)
```

```python
import jax
import jax.numpy as jnp
from jax import lax
from jax.experimental import pallas as pl
from jax.experimental.pallas import tpu as pltpu
from jax.sharding import PartitionSpec as P

eps_norm = 1e-06
f32 = jnp.float32
bf16 = jnp.bfloat16
MESH = pl.DeviceIdType.MESH
NT = (((1,), (1,)), ((), ()))
TN = (((0,), (0,)), ((), ()))


def mm(a, b):
    return jnp.dot(a, b, preferred_element_type=f32)


def split2(x):
    hi = x.astype(bf16)
    return hi, (x - hi.astype(f32)).astype(bf16)


def split3(x):
    hi, rest = x.astype(bf16), None
    rest = x - hi.astype(f32)
    mid = rest.astype(bf16)
    return hi, mid, (rest - mid.astype(f32)).astype(bf16)


def wide(x):
    return jnp.concatenate(split2(x), axis=1)


def square(x):
    row = jnp.concatenate(split2(x), axis=1)
    return jnp.concatenate([row, row], axis=0)


def mm4(a_wide, b_square, size):
    both = mm(a_wide, b_square)
    return both[:, :size] + both[:, size:]


def square_t(x):
    hi, lo = split2(x)
    return jnp.concatenate(
        [jnp.concatenate([hi, hi], axis=1), jnp.concatenate([lo, lo], axis=1)], axis=0
    )


def iotas(r, c):
    return (
        lax.broadcasted_iota(jnp.int32, (r, c), 0),
        lax.broadcasted_iota(jnp.int32, (r, c), 1),
    )


def nt(a, b):
    return lax.dot_general(a, b, NT, preferred_element_type=f32)


def kernel(inner, count, k_ref, v_ref, q_ref, lg_ref, gate_ref, gain_ref, o_ref,
           maps, gath, pre, pre_sq, total, r_ref, lo_ref, x_in, y_in, x_out, starts, states,
           map_send, map_recv, x_send, x_recv, y_send, y_recv, back_send, back_recv):
    steps = k_ref.shape[0]
    toks = q_ref.shape[0]
    heads = lg_ref.shape[0]
    d = k_ref.shape[1] // heads
    half = steps // 2
    own = heads // 4
    quads = count // 4
    direct = quads == 4

    me = lax.axis_index("outer") * inner + lax.axis_index("inner")
    pos = me % 4
    quad = me // 4
    places = [pos + 1 - 2 * (pos % 2), pos + 2 - 4 * (pos // 2), 3 - pos]

    def place(i):
        return {"outer": i // inner, "inner": i % inner}

    barrier = pltpu.get_barrier_semaphore()

    def greet(i):
        pl.semaphore_signal(barrier, inc=1, device_id=place(i), device_id_type=MESH)

    for at in places:
        greet(4 * quad + at)

    @pl.when(quad >= 1)
    def _():
        greet(me - 4)

    if direct:
        @pl.when(quad >= 2)
        def _():
            greet(me - 8)

    def greeted():
        hops = 2 if direct else 1

        for more in range(hops + 1):
            @pl.when((quad < quads - hops) if more == hops else (quad == quads - 1 - more))
            def _():
                pl.semaphore_wait(barrier, 3 + more)

    def remote(src, dst, send, recv, target):
        return pltpu.make_async_remote_copy(
            src_ref=src, dst_ref=dst, send_sem=send, recv_sem=recv,
            device_id=place(target), device_id_type=MESH,
        )

    def map_copy(j, k):
        return remote(maps.at[4 * j + places[k]], gath.at[pos, j], map_send.at[j, k], map_recv.at[j, k],
                      4 * quad + places[k])

    def back_copy(j, k):
        return remote(starts.at[j, places[k]], states.at[4 * j + pos], back_send.at[j, k], back_recv.at[j, k],
                      4 * quad + places[k])

    def x_copy(j, src, hop):
        return remote(src, x_in.at[j], x_send.at[j, hop - 1], x_recv.at[j], me + 4 * hop)

    def y_copy(j):
        return remote(total.at[j], y_in.at[j], y_send.at[j], y_recv.at[j], me + 4)

    i_st, j_tk = iotas(steps, toks)
    tri_steps = (j_tk <= i_st // 2).astype(f32).astype(bf16)
    i_tk, j_tk2 = iotas(toks, toks)
    tri_toks = (j_tk2 <= i_tk).astype(f32).astype(bf16)
    lgs = split3(lg_ref[...])
    c_col = sum(nt(tri_steps, p) for p in lgs)
    q_col = sum(nt(tri_toks, p) for p in lgs)
    c_row = sum(nt(p, tri_steps) for p in lgs)
    ii, jj = iotas(steps, steps)
    strict = ii > jj
    it, jt = iotas(toks, steps)
    visible = jt <= 2 * it + 1
    hi_, hj_ = iotas(half, half)
    eye = (hi_ == hj_).astype(f32)
    di, dj = iotas(d, d)
    eye_d = (di == dj).astype(f32)
    ones8 = jnp.ones((8, d), bf16)
    onesd = jnp.ones((d, d), bf16)

    ks, nrow, solved = {}, {}, {}
    for turn in range(own):
        hs = range(4 * turn, 4 * turn + 4)
        lower, ncol, invs = {}, {}, {}
        for h in hs:
            k = k_ref[:, h * d : (h + 1) * d]
            kf = k.astype(f32)
            sq = split2(kf * kf)
            n_c = lax.rsqrt(sum(mm(p, onesd) for p in sq) + eps_norm)
            n_r = lax.rsqrt(sum(nt(ones8, p) for p in sq) + eps_norm)[:1]
            gram = nt(k, k)
            gap = jnp.where(strict, c_col[:, h : h + 1] - c_row[h : h + 1, :], 0.0)
            n_cc = jnp.concatenate([n_c] * (steps // d), axis=1)
            low = jnp.where(strict, jnp.exp(gap) * gram * (2.0 * n_r) * n_cc, 0.0)
            ks[h], lower[h], ncol[h], nrow[h] = k, low, n_c, n_r
            diag = [low[:half, :half], low[half:, half:]]
            m = hi_ // 2 == hj_ // 2
            invs[h] = [eye - jnp.where(m, x, 0.0) for x in diag]
        b = 2
        while b < half:
            m = (hi_ // (2 * b) == hj_ // (2 * b)) & ((hi_ // b) % 2 == 1) & ((hj_ // b) % 2 == 0)
            for h in hs:
                for s in range(2):
                    block = lower[h][s * half : (s + 1) * half, s * half : (s + 1) * half]
                    off = jnp.where(m, block, 0.0)
                    iww = wide(invs[h][s])
                    t = mm4(iww, square(off), half)
                    invs[h][s] = invs[h][s] - mm4(wide(t), jnp.concatenate([iww, iww], axis=0), half)
            b *= 2
        for h in hs:
            t = mm4(wide(invs[h][1]), square(lower[h][half:, :half]), half)
            c21 = -mm4(wide(t), square(invs[h][0]), half)
            minv = jnp.concatenate(
                [
                    jnp.concatenate([invs[h][0], jnp.zeros((half, half), f32)], axis=1),
                    jnp.concatenate([c21, invs[h][1]], axis=1),
                ],
                axis=0,
            )
            k = ks[h]
            v = v_ref[:, h * d : (h + 1) * d]
            y = sum(mm(p, v) for p in split2(minv))
            grow = jnp.exp(c_row[h : h + 1, :]) * nrow[h]
            w = sum(mm(p, k) for p in split2(minv * grow))
            last = c_col[steps - 1 :, h : h + 1]
            tail = jnp.exp(last - c_col[:, h : h + 1]) * (2.0 * ncol[h])
            kt = jnp.transpose(k.astype(f32)).astype(bf16)
            wy = jnp.concatenate([tail * w, tail * y], axis=1)
            ab = jnp.transpose(sum(mm(kt, p) for p in split2(wy)))
            maps[h] = jnp.concatenate([jnp.exp(last) * eye_d - ab[:d], ab[d:]], axis=0)
            solved[h] = (y, w)
        if turn == 0:
            greeted()
        for k in (2, 0, 1):
            map_copy(turn, k).start()

    for h in range(heads):
        k = ks[h]
        y, w = solved[h]
        q = q_ref[:, h * d : (h + 1) * d]
        qc = q_col[:, h : h + 1]
        qgap = jnp.where(visible, qc - c_row[h : h + 1, :], 0.0)
        pairs = jnp.where(visible, jnp.exp(qgap) * nt(q, k) * (2.0 * nrow[h]), 0.0)
        p_hi, p_lo = split2(pairs)
        x_hi, x_lo = split2(jnp.concatenate([y, w], axis=1))
        px = mm(p_hi, x_hi) + mm(p_lo, x_hi) + mm(p_hi, x_lo)
        lo_ref[h] = px[:, :d]
        r_ref[h] = wide(jnp.exp(qc) * q.astype(f32) - px[:, d:])

    def add_low(both, low):
        return jnp.concatenate([both[:d], both[d:] + low], axis=0)

    def compose(j):
        gath[pos, j] = maps[4 * j + pos]
        for k in range(3):
            map_copy(j, k).wait_recv()
        m = [gath[i, j] for i in range(4)]
        second = square(m[1][:d])
        third = square(m[2][:d])
        m01 = add_low(mm4(wide(m[0]), second, d), m[1][d:])
        m23 = add_low(mm4(wide(m[2]), square(m[3][:d]), d), m[3][d:])
        w01 = wide(m01)
        whole = add_low(mm4(w01, square(m23[:d]), d), m23[d:])
        total[j] = whole

        if direct:
            @pl.when(quad == 0)
            def _():
                x_copy(j, total.at[j, pl.ds(d, d)], 1).start()
                x_copy(j, total.at[j, pl.ds(d, d)], 2).start()

            @pl.when((quad == 1) | (quad == 2))
            def _():
                y_copy(j).start()

        m012 = add_low(mm4(w01, third, d), m[2][d:])
        for i, x in enumerate((m[0], m01, m012)):
            pre_sq[j, i] = square(x[:d])
            pre[j, i] = x[d:]

    def give(j, start):
        starts[j, 0] = start
        rows = wide(start)
        for i in range(3):
            starts[j, i + 1] = mm4(rows, pre_sq[j, i], d) + pre[j, i]
        for k in (2, 0, 1):
            back_copy(j, k).start()

    def pass_on(j, start, hop):
        x_out[j] = mm4(wide(start), square(total[j, :d]), d) + total[j, d:]
        x_copy(j, x_out.at[j], hop).start()

    for j in range(own):
        compose(j)

        @pl.when(quad == 0)
        def _():
            if not direct:
                x_copy(j, total.at[j, pl.ds(d, d)], 1).start()
            give(j, jnp.zeros((d, d), f32))

    for j in range(own):
        if direct:
            @pl.when(quad == 1)
            def _():
                x_copy(j, x_out.at[j], 1).wait_recv()
                pass_on(j, x_in[j], 2)
                give(j, x_in[j])

            @pl.when(quad >= 2)
            def _():
                y_copy(j).wait_recv()
                x_copy(j, x_out.at[j], 1).wait_recv()
                give(j, mm4(wide(x_in[j]), square(y_in[j, :d]), d) + y_in[j, d:])
        else:
            @pl.when(quad >= 1)
            def _():
                x_copy(j, x_out.at[j], 1).wait_recv()

                @pl.when(quad < quads - 1)
                def _():
                    pass_on(j, x_in[j], 1)

                give(j, x_in[j])

    gain = gain_ref[...]

    def readout(h, state_t):
        both = nt(r_ref[h], square_t(state_t))
        out = both[:, :d] + both[:, d:] + lo_ref[h]
        scale = lax.rsqrt(jnp.mean(out * out, axis=-1, keepdims=True) + eps_norm)
        cols = pl.ds(pl.multiple_of(h * d, d), d)
        g = gate_ref[:, cols].astype(f32)
        o_ref[:, cols] = (out * scale * gain * (g / (1.0 + jnp.exp(-g)))).astype(bf16)

    for j in range(own):
        readout(4 * j + pos, starts[j, pos])
        for k in range(3):
            back_copy(j, k).wait_recv()
            readout(4 * j + places[k], states[4 * j + places[k]])

    for j in range(own):
        for k in range(3):
            map_copy(j, k).wait_send()
            back_copy(j, k).wait_send()
        if direct:
            @pl.when(quad == 0)
            def _():
                x_copy(j, total.at[j, pl.ds(d, d)], 1).wait_send()

            @pl.when(quad < 2)
            def _():
                x_copy(j, x_out.at[j], 2).wait_send()

            @pl.when((quad == 1) | (quad == 2))
            def _():
                y_copy(j).wait_send()
        else:
            @pl.when(quad < quads - 1)
            def _():
                x_copy(j, x_out.at[j], 1).wait_send()


def vmem_specs(n):
    return [pl.BlockSpec(memory_space=pltpu.VMEM)] * n


def solution(mesh):
    inner = mesh.shape["inner"]
    count = inner * mesh.shape["outer"]
    assert count % 4 == 0

    def local(queries, keys, values, log_gate, out_gate, norm_gain):
        toks, width = queries.shape
        heads = log_gate.shape[1]
        d = width // heads
        steps = 2 * toks
        own = heads // 4
        dma = pltpu.SemaphoreType.DMA
        return pl.pallas_call(
            lambda *refs: kernel(inner, count, *refs),
            out_shape=jax.ShapeDtypeStruct((toks, width), bf16),
            in_specs=vmem_specs(6),
            out_specs=vmem_specs(1)[0],
            scratch_shapes=[
                pltpu.VMEM((heads, 2 * d, d), f32),
                pltpu.VMEM((4, own, 2 * d, d), f32),
                pltpu.VMEM((own, 3, d, d), f32),
                pltpu.VMEM((own, 3, 2 * d, 2 * d), bf16),
                pltpu.VMEM((own, 2 * d, d), f32),
                pltpu.VMEM((heads, d, 2 * d), bf16),
                pltpu.VMEM((heads, d, d), f32),
                pltpu.VMEM((own, d, d), f32),
                pltpu.VMEM((own, 2 * d, d), f32),
                pltpu.VMEM((own, d, d), f32),
                pltpu.VMEM((own, 4, d, d), f32),
                pltpu.VMEM((heads, d, d), f32),
                dma((own, 3)), dma((own, 3)), dma((own, 2)), dma((own,)),
                dma((own,)), dma((own,)), dma((own, 3)), dma((own, 3)),
            ],
            compiler_params=pltpu.CompilerParams(
                collective_id=0, has_side_effects=True, vmem_limit_bytes=48 << 20
            ),
            name="delta_product",
        )(keys.reshape(steps, width), values.reshape(steps, width), queries, log_gate.T,
          out_gate, norm_gain.reshape(1, d))

    spec = P(("groups", "outer", "inner"), None)
    spec3 = P(("groups", "outer", "inner"), None, None)
    return jax.shard_map(
        local, mesh=mesh, in_specs=(spec, spec3, spec3, spec, spec, P()), out_specs=spec, check_vma=False
    )
```

```python
import jax
import jax.numpy as jnp
from jax import lax
from jax.experimental import pallas as pl
from jax.experimental.pallas import tpu as pltpu
from jax.sharding import PartitionSpec as P

eps_norm = 1e-06
f32 = jnp.float32
bf16 = jnp.bfloat16
MESH = pl.DeviceIdType.MESH
NT = (((1,), (1,)), ((), ()))
TN = (((0,), (0,)), ((), ()))


def mm(a, b):
    return jnp.dot(a, b, preferred_element_type=f32)


def split2(x):
    hi = x.astype(bf16)
    return hi, (x - hi.astype(f32)).astype(bf16)


def split3(x):
    hi, rest = x.astype(bf16), None
    rest = x - hi.astype(f32)
    mid = rest.astype(bf16)
    return hi, mid, (rest - mid.astype(f32)).astype(bf16)


def wide(x):
    return jnp.concatenate(split2(x), axis=1)


def square(x):
    row = jnp.concatenate(split2(x), axis=1)
    return jnp.concatenate([row, row], axis=0)


def mm4(a_wide, b_square, size):
    both = mm(a_wide, b_square)
    return both[:, :size] + both[:, size:]


def twice(x):
    return jnp.concatenate([x, x], axis=0)


def square_t(x):
    hi, lo = split2(x)
    return jnp.concatenate(
        [jnp.concatenate([hi, hi], axis=1), jnp.concatenate([lo, lo], axis=1)], axis=0
    )


def iotas(r, c):
    return (
        lax.broadcasted_iota(jnp.int32, (r, c), 0),
        lax.broadcasted_iota(jnp.int32, (r, c), 1),
    )


def nt(a, b):
    return lax.dot_general(a, b, NT, preferred_element_type=f32)


def kernel(inner, count, k_hbm, v_hbm, q_hbm, lg_hbm, gate_hbm, gain_hbm, o_ref,
           k_ref, v_ref, k_rows, v_rows, q_ref, lg_ref, gate_ref, gain_ref, in_sems, maps, gath, pre, pre_sq, total, r_ref, lo_ref, x_in, y_in, x_out, starts, states,
           map_send, map_recv, x_send, x_recv, y_send, y_recv, back_send, back_recv):
    toks, width = q_ref.shape
    steps = 2 * toks
    heads = lg_ref.shape[0]
    d = width // heads
    half = steps // 2
    own = heads // 4
    quads = count // 4
    direct = quads == 4

    me = lax.axis_index("outer") * inner + lax.axis_index("inner")
    pos = me % 4
    quad = me // 4
    places = [pos + 1 - 2 * (pos % 2), pos + 2 - 4 * (pos // 2), 3 - pos]

    def place(i):
        return {"outer": i // inner, "inner": i % inner}

    barrier = pltpu.get_barrier_semaphore()

    def greet(i):
        pl.semaphore_signal(barrier, inc=1, device_id=place(i), device_id_type=MESH)

    for at in places:
        greet(4 * quad + at)

    @pl.when(quad >= 1)
    def _():
        greet(me - 4)

    if direct:
        @pl.when(quad >= 2)
        def _():
            greet(me - 8)

    def greeted():
        hops = 2 if direct else 1

        for more in range(hops + 1):
            @pl.when((quad < quads - hops) if more == hops else (quad == quads - 1 - more))
            def _():
                pl.semaphore_wait(barrier, 3 + more)

    def remote(src, dst, send, recv, target):
        return pltpu.make_async_remote_copy(
            src_ref=src, dst_ref=dst, send_sem=send, recv_sem=recv,
            device_id=place(target), device_id_type=MESH,
        )

    def map_copy(h):
        return remote(maps.at[h], gath.at[pos, h // 4], map_send.at[h], map_recv.at[h // 4, pos],
                      4 * quad + h % 4)

    def map_from(j, k):
        return remote(maps.at[0], gath.at[places[k], j], map_send.at[0], map_recv.at[j, places[k]],
                      4 * quad + places[k])

    def back_copy(j, k):
        return remote(starts.at[j, places[k]], states.at[4 * j + pos], back_send.at[j, k], back_recv.at[j, k],
                      4 * quad + places[k])

    def x_copy(j, src, hop):
        return remote(src, x_in.at[j], x_send.at[j, hop - 1], x_recv.at[j], me + 4 * hop)

    def y_copy(j):
        return remote(total.at[j], y_in.at[j], y_send.at[j], y_recv.at[j], me + 4)

    def fetch(h, which):
        src, dst = ((k_hbm, k_ref), (v_hbm, v_ref))[which]
        cols = pl.ds(h * d, d)
        return pltpu.make_async_copy(src.at[:, :, cols], dst.at[:, :, cols], in_sems.at[2 * h + which])

    others = [
        pltpu.make_async_copy(src, dst, in_sems.at[2 * heads + i])
        for i, (src, dst) in enumerate(
            ((lg_hbm, lg_ref), (q_hbm, q_ref), (gate_hbm, gate_ref), (gain_hbm, gain_ref))
        )
    ]
    others[0].start()
    for h in range(heads):
        fetch(h, 0).start()
        fetch(h, 1).start()
    for copy in others[1:]:
        copy.start()

    i_st, j_tk = iotas(steps, toks)
    tri_steps = (j_tk <= i_st // 2).astype(f32).astype(bf16)
    i_tk, j_tk2 = iotas(toks, toks)
    tri_toks = (j_tk2 <= i_tk).astype(f32).astype(bf16)
    others[0].wait()
    lgs = split3(lg_ref[...])
    c_col = sum(nt(tri_steps, p) for p in lgs)
    q_col = sum(nt(tri_toks, p) for p in lgs)
    c_row = sum(nt(p, tri_steps) for p in lgs)
    it, jt = iotas(toks, steps)
    visible = jt <= 2 * it + 1
    hi_, hj_ = iotas(half, half)
    eye = (hi_ == hj_).astype(f32)
    di, dj = iotas(d, d)
    levels = [2**i for i in range(1, half.bit_length() - 1)]
    corner = {
        b: ((hi_ // (2 * b) == hj_ // (2 * b)) & ((hi_ // b) % 2 == 1) & ((hj_ // b) % 2 == 0)).astype(f32).astype(bf16)
        for b in levels
    }
    below = hi_ > hj_
    close = hi_ // 2 == hj_ // 2
    eye_d = (di == dj).astype(f32)
    ones8 = jnp.ones((8, d), bf16)
    onesd = jnp.ones((d, d), bf16)

    nrow, solved = {}, {}
    keeps = {b: jnp.concatenate([corner[b]] * 2, axis=1) for b in levels}

    def solve(h):
        k_rows[:, h * d : (h + 1) * d] = k_ref[:, :, h * d : (h + 1) * d].reshape(steps, d)
        v_rows[:, h * d : (h + 1) * d] = v_ref[:, :, h * d : (h + 1) * d].reshape(steps, d)
        k = k_rows[:, h * d : (h + 1) * d]
        kf = k.astype(f32)
        sq = split2(kf * kf)
        yield
        n_c = lax.rsqrt(sum(mm(p, onesd) for p in sq) + eps_norm)
        n_r = lax.rsqrt(sum(nt(ones8, p) for p in sq) + eps_norm)[:1]
        nrow[h] = n_r
        c_h = jnp.broadcast_to(c_col[:, h : h + 1], (steps, d))
        row = c_row[h : h + 1, :]
        yield

        def coupled(i, j):
            at, to = slice(i * half, (i + 1) * half), slice(j * half, (j + 1) * half)
            gap = jnp.minimum(c_h[at] - row[:, to], 0.0)
            return jnp.exp(gap) * nt(k[at], k[to]) * (2.0 * n_r[:, to]) * n_c[at]

        diag = [jnp.where(below, coupled(i, i), 0.0) for i in range(2)]
        joint = coupled(1, 0)
        yield
        tri = [wide(x) for x in diag]
        invs = [eye - jnp.where(close, x, 0.0) for x in diag]
        wides = [wide(x) for x in invs]
        yield
        for b in levels:
            spans = [(i, i + b) for i in range(0, half, b)]

            def odd(x):
                return jnp.concatenate([x[p:q] for p, q in spans[1::2]], axis=0)

            def mixed(x, new):
                return jnp.concatenate(
                    [x[p:q] if n % 2 == 0 else new[(n // 2) * b : (n // 2 + 1) * b] for n, (p, q) in enumerate(spans)],
                    axis=0,
                )

            olds = invs if b < 8 else [odd(x) for x in invs]
            if b < 8:
                rows = wides
            elif b < 16:
                rows = [wide(x) for x in olds]
            else:
                rows = [odd(x) for x in wides]
            ts = [mm4(rows[i], twice(tri[i] * keeps[b]), half) for i in range(2)]
            yield
            ts = [wide(t) for t in ts]
            news = [olds[i] - mm4(ts[i], twice(wides[i]), half) for i in range(2)]
            yield
            if b < 8:
                invs = news
                wides = [wide(x) for x in invs]
            else:
                invs = [mixed(x, new) for x, new in zip(invs, news)]
                if b < 16:
                    wides = [wide(x) for x in invs]
                else:
                    wides = [mixed(x, wide(new)) for x, new in zip(wides, news)]
        first, second = wides
        t = mm4(second, square(joint), half)
        k = k_rows[:, h * d : (h + 1) * d].astype(f32)
        v = v_rows[:, h * d : (h + 1) * d]
        yield
        rhs = jnp.concatenate([v, wide(jnp.exp(c_h) * n_c * k)], axis=1)
        across = wide(-mm4(wide(t), twice(first), half))
        top = mm(first, twice(rhs[:half]))
        yield
        low = mm(jnp.concatenate([across, second], axis=1),
                 jnp.concatenate([twice(rhs[:half]), twice(rhs[half:])], axis=0))
        last = c_col[steps - 1 :, h : h + 1]
        tail = jnp.exp(c_h[steps - 1 :] - c_h) * (2.0 * n_c)
        t_hi, t_lo = split2(jnp.transpose(tail * k))
        yield
        x = jnp.concatenate([top, low], axis=0)
        x_hi, x_lo = split2(jnp.concatenate([x[:, :d], x[:, d : 2 * d] + x[:, 2 * d :]], axis=1))
        solved[h] = (x_hi, x_lo)
        yield
        ba = mm(t_hi, x_hi) + mm(t_lo, x_hi) + mm(t_hi, x_lo)
        yield
        ba = jnp.transpose(ba)
        maps[h] = jnp.concatenate([jnp.exp(last) * eye_d - ba[d:], ba[:d]], axis=0)

    def inside(h):
        k = k_rows[:, h * d : (h + 1) * d]
        x_hi, x_lo = solved[h]
        q = q_ref[:, h * d : (h + 1) * d]
        qc = q_col[:, h : h + 1]
        qgap = jnp.minimum(qc - c_row[h : h + 1, :], 0.0)
        pairs = jnp.where(visible, jnp.exp(qgap) * nt(q, k) * (2.0 * nrow[h]), 0.0)
        yield
        p_hi, p_lo = split2(pairs)
        px = mm(p_hi, x_hi) + mm(p_lo, x_hi) + mm(p_hi, x_lo)
        yield
        lo_ref[h] = px[:, :d]
        r_ref[h] = wide(jnp.exp(qc) * q.astype(f32) - px[:, d:])

    def together(works):
        works = list(works)
        while works:
            works = [work for work in works if next(work, works) is not works]

    groups = ((0, 1, 2, 3), (4, 5, 6, 7))
    for turn, hs in enumerate(groups):
        for h in hs:
            fetch(h, 0).wait()
            fetch(h, 1).wait()
        together(solve(h) for h in hs)
        if turn == 0:
            greeted()
        for h in hs:
            @pl.when(pos != h % 4)
            def _():
                map_copy(h).start()

    for copy in others[1:]:
        copy.wait()
    for hs in groups:
        together(inside(h) for h in hs)

    def add_low(both, low):
        return jnp.concatenate([both[:d], both[d:] + low], axis=0)

    def compose(j):
        gath[pos, j] = maps[4 * j + pos]
        for k in range(3):
            map_from(j, k).wait_recv()
        m = [gath[i, j] for i in range(4)]
        second = square(m[1][:d])
        third = square(m[2][:d])
        m01 = add_low(mm4(wide(m[0]), second, d), m[1][d:])
        m23 = add_low(mm4(wide(m[2]), square(m[3][:d]), d), m[3][d:])
        w01 = wide(m01)
        whole = add_low(mm4(w01, square(m23[:d]), d), m23[d:])
        total[j] = whole

        if direct:
            @pl.when(quad == 0)
            def _():
                x_copy(j, total.at[j, pl.ds(d, d)], 1).start()
                x_copy(j, total.at[j, pl.ds(d, d)], 2).start()

            @pl.when((quad == 1) | (quad == 2))
            def _():
                y_copy(j).start()

        m012 = add_low(mm4(w01, third, d), m[2][d:])
        for i, x in enumerate((m[0], m01, m012)):
            pre_sq[j, i] = square(x[:d])
            pre[j, i] = x[d:]

    def give(j, start):
        starts[j, 0] = start
        rows = wide(start)
        for i in range(3):
            starts[j, i + 1] = mm4(rows, pre_sq[j, i], d) + pre[j, i]
        for k in (2, 0, 1):
            back_copy(j, k).start()

    def pass_on(j, start, hop):
        x_out[j] = mm4(wide(start), square(total[j, :d]), d) + total[j, d:]
        x_copy(j, x_out.at[j], hop).start()

    for j in range(own):
        compose(j)

        @pl.when(quad == 0)
        def _():
            if not direct:
                x_copy(j, total.at[j, pl.ds(d, d)], 1).start()
            give(j, jnp.zeros((d, d), f32))

    for j in range(own):
        if direct:
            @pl.when(quad == 1)
            def _():
                x_copy(j, x_out.at[j], 1).wait_recv()
                pass_on(j, x_in[j], 2)
                give(j, x_in[j])

            @pl.when(quad >= 2)
            def _():
                y_copy(j).wait_recv()
                x_copy(j, x_out.at[j], 1).wait_recv()
                give(j, mm4(wide(x_in[j]), square(y_in[j, :d]), d) + y_in[j, d:])
        else:
            @pl.when(quad >= 1)
            def _():
                x_copy(j, x_out.at[j], 1).wait_recv()

                @pl.when(quad < quads - 1)
                def _():
                    pass_on(j, x_in[j], 1)

                give(j, x_in[j])

    gain = gain_ref[...]

    def readout(h, state_t):
        both = nt(r_ref[h], square_t(state_t))
        out = both[:, :d] + both[:, d:] + lo_ref[h]
        scale = lax.rsqrt(jnp.mean(out * out, axis=-1, keepdims=True) + eps_norm)
        cols = pl.ds(pl.multiple_of(h * d, d), d)
        g = gate_ref[:, cols].astype(f32)
        o_ref[:, cols] = (out * scale * gain * (g / (1.0 + jnp.exp(-g)))).astype(bf16)

    for h in range(heads):
        @pl.when(pos != h % 4)
        def _():
            map_copy(h).wait_send()

    for j in range(own):
        readout(4 * j + pos, starts[j, pos])
        for k in range(3):
            back_copy(j, k).wait_recv()
            readout(4 * j + places[k], states[4 * j + places[k]])

    for j in range(own):
        for k in range(3):
            back_copy(j, k).wait_send()
        if direct:
            @pl.when(quad == 0)
            def _():
                x_copy(j, total.at[j, pl.ds(d, d)], 1).wait_send()

            @pl.when(quad < 2)
            def _():
                x_copy(j, x_out.at[j], 2).wait_send()

            @pl.when((quad == 1) | (quad == 2))
            def _():
                y_copy(j).wait_send()
        else:
            @pl.when(quad < quads - 1)
            def _():
                x_copy(j, x_out.at[j], 1).wait_send()


def solution(mesh):
    inner = mesh.shape["inner"]
    count = inner * mesh.shape["outer"]
    assert count % 4 == 0

    def local(queries, keys, values, log_gate, out_gate, norm_gain):
        toks, width = queries.shape
        heads = log_gate.shape[1]
        d = width // heads
        own = heads // 4
        dma = pltpu.SemaphoreType.DMA
        return pl.pallas_call(
            lambda *refs: kernel(inner, count, *refs),
            out_shape=jax.ShapeDtypeStruct((toks, width), bf16),
            in_specs=[pl.BlockSpec(memory_space=pltpu.HBM)] * 6,
            out_specs=pl.BlockSpec(memory_space=pltpu.VMEM),
            scratch_shapes=[
                pltpu.VMEM((toks, 2, width), bf16),
                pltpu.VMEM((toks, 2, width), bf16),
                pltpu.VMEM((2 * toks, width), bf16),
                pltpu.VMEM((2 * toks, width), bf16),
                pltpu.VMEM((toks, width), bf16),
                pltpu.VMEM((heads, toks), f32),
                pltpu.VMEM((toks, width), bf16),
                pltpu.VMEM((1, d), f32),
                dma((2 * heads + 4,)),
                pltpu.VMEM((heads, 2 * d, d), f32),
                pltpu.VMEM((4, own, 2 * d, d), f32),
                pltpu.VMEM((own, 3, d, d), f32),
                pltpu.VMEM((own, 3, 2 * d, 2 * d), bf16),
                pltpu.VMEM((own, 2 * d, d), f32),
                pltpu.VMEM((heads, d, 2 * d), bf16),
                pltpu.VMEM((heads, d, d), f32),
                pltpu.VMEM((own, d, d), f32),
                pltpu.VMEM((own, 2 * d, d), f32),
                pltpu.VMEM((own, d, d), f32),
                pltpu.VMEM((own, 4, d, d), f32),
                pltpu.VMEM((heads, d, d), f32),
                dma((heads,)), dma((own, 4)), dma((own, 2)), dma((own,)),
                dma((own,)), dma((own,)), dma((own, 3)), dma((own, 3)),
            ],
            compiler_params=pltpu.CompilerParams(
                collective_id=0, has_side_effects=True, vmem_limit_bytes=48 << 20
            ),
            name="delta_product",
        )(*[pltpu.with_memory_space_constraint(x, pltpu.HBM) for x in (keys, values, queries, log_gate.T, out_gate, norm_gain.reshape(1, d))])

    spec = P(("groups", "outer", "inner"), None)
    spec3 = P(("groups", "outer", "inner"), None, None)
    return jax.shard_map(
        local, mesh=mesh, in_specs=(spec, spec3, spec3, spec, spec, P()), out_specs=spec, check_vma=False
    )
```

```python
import jax
import jax.numpy as jnp
from jax import lax
from jax.experimental import pallas as pl
from jax.experimental.pallas import tpu as pltpu
from jax.sharding import PartitionSpec as P

eps_norm = 1e-06
f32 = jnp.float32
bf16 = jnp.bfloat16
MESH = pl.DeviceIdType.MESH
NT = (((1,), (1,)), ((), ()))
TN = (((0,), (0,)), ((), ()))


def mm(a, b):
    return jnp.dot(a, b, preferred_element_type=f32)


def split2(x):
    hi = x.astype(bf16)
    return hi, (x - hi.astype(f32)).astype(bf16)


def split3(x):
    hi, rest = x.astype(bf16), None
    rest = x - hi.astype(f32)
    mid = rest.astype(bf16)
    return hi, mid, (rest - mid.astype(f32)).astype(bf16)


def wide(x):
    return jnp.concatenate(split2(x), axis=1)


def square(x):
    row = jnp.concatenate(split2(x), axis=1)
    return jnp.concatenate([row, row], axis=0)


def mm4(a_wide, b_square, size):
    both = mm(a_wide, b_square)
    return both[:, :size] + both[:, size:]


def twice(x):
    return jnp.concatenate([x, x], axis=0)


def square_t(x):
    hi, lo = split2(x)
    return jnp.concatenate(
        [jnp.concatenate([hi, hi], axis=1), jnp.concatenate([lo, lo], axis=1)], axis=0
    )


def iotas(r, c):
    return (
        lax.broadcasted_iota(jnp.int32, (r, c), 0),
        lax.broadcasted_iota(jnp.int32, (r, c), 1),
    )


def nt(a, b):
    return lax.dot_general(a, b, NT, preferred_element_type=f32)


def kernel(inner, count, k_hbm, v_hbm, q_hbm, lg_hbm, gate_hbm, gain_hbm, o_ref,
           k_ref, v_ref, k_rows, v_rows, q_ref, lg_ref, gate_ref, gain_ref, in_sems, maps, gath, pre, pre_sq, total, r_ref, lo_ref, x_in, y_in, x_out, starts, states,
           map_send, map_recv, x_send, x_recv, y_send, y_recv, back_send, back_recv, turn_sem):
    toks, width = q_ref.shape
    steps = 2 * toks
    heads = lg_ref.shape[0]
    d = width // heads
    half = steps // 2
    own = heads // 4
    quads = count // 4
    direct = quads == 4

    me = lax.axis_index("outer") * inner + lax.axis_index("inner")
    pos = me % 4
    quad = me // 4
    places = [pos + 1 - 2 * (pos % 2), pos + 2 - 4 * (pos // 2), 3 - pos]

    def place(i):
        return {"outer": i // inner, "inner": i % inner}

    barrier = pltpu.get_barrier_semaphore()

    def greet(i):
        pl.semaphore_signal(barrier, inc=1, device_id=place(i), device_id_type=MESH)

    for at in places:
        greet(4 * quad + at)

    @pl.when(quad >= 1)
    def _():
        greet(me - 4)

    if direct:
        @pl.when(quad >= 2)
        def _():
            greet(me - 8)

    def greeted():
        hops = 2 if direct else 1

        for more in range(hops + 1):
            @pl.when((quad < quads - hops) if more == hops else (quad == quads - 1 - more))
            def _():
                pl.semaphore_wait(barrier, 3 + more)

    def remote(src, dst, send, recv, target):
        return pltpu.make_async_remote_copy(
            src_ref=src, dst_ref=dst, send_sem=send, recv_sem=recv,
            device_id=place(target), device_id_type=MESH,
        )

    def map_copy(j, k):
        h = 4 * j + places[k]
        return remote(maps.at[h], gath.at[pos, j], map_send.at[h], map_recv.at[j, pos], 4 * quad + places[k])

    def map_from(j, k):
        return remote(maps.at[0], gath.at[places[k], j], map_send.at[0], map_recv.at[j, places[k]],
                      4 * quad + places[k])

    def back_copy(j, k):
        return remote(starts.at[j, places[k]], states.at[4 * j + pos], back_send.at[j, k], back_recv.at[j, k],
                      4 * quad + places[k])

    def x_copy(j, src, hop):
        return remote(src, x_in.at[j], x_send.at[j, hop - 1], x_recv.at[j], me + 4 * hop)

    def y_copy(j):
        return remote(total.at[j], y_in.at[j], y_send.at[j], y_recv.at[j], me + 4)

    def fetch(h, which):
        src, dst = ((k_hbm, k_ref), (v_hbm, v_ref))[which]
        cols = pl.ds(h * d, d)
        return pltpu.make_async_copy(src.at[:, :, cols], dst.at[:, :, cols], in_sems.at[2 * h + which])

    others = [
        pltpu.make_async_copy(src, dst, in_sems.at[2 * heads + i])
        for i, (src, dst) in enumerate(
            ((lg_hbm, lg_ref), (q_hbm, q_ref), (gate_hbm, gate_ref), (gain_hbm, gain_ref))
        )
    ]
    others[0].start()
    for h in range(heads):
        fetch(h, 0).start()
        fetch(h, 1).start()
    for copy in others[1:]:
        copy.start()

    i_st, j_tk = iotas(steps, toks)
    tri_steps = (j_tk <= i_st // 2).astype(f32).astype(bf16)
    i_tk, j_tk2 = iotas(toks, toks)
    tri_toks = (j_tk2 <= i_tk).astype(f32).astype(bf16)
    others[0].wait()
    lgs = split3(lg_ref[...])
    c_col = sum(nt(tri_steps, p) for p in lgs)
    q_col = sum(nt(tri_toks, p) for p in lgs)
    c_row = sum(nt(p, tri_steps) for p in lgs)
    it, jt = iotas(toks, steps)
    visible = jt <= 2 * it + 1
    hi_, hj_ = iotas(half, half)
    eye = (hi_ == hj_).astype(f32)
    di, dj = iotas(d, d)
    levels = [2**i for i in range(1, half.bit_length() - 1)]
    corner = {
        b: ((hi_ // (2 * b) == hj_ // (2 * b)) & ((hi_ // b) % 2 == 1) & ((hj_ // b) % 2 == 0)).astype(f32).astype(bf16)
        for b in levels
    }
    below = hi_ > hj_
    close = hi_ // 2 == hj_ // 2
    eye_d = (di == dj).astype(f32)
    ones8 = jnp.ones((8, d), bf16)
    onesd = jnp.ones((d, d), bf16)

    nrow, solved = {}, {}
    keeps = {b: jnp.concatenate([corner[b]] * 2, axis=1) for b in levels}

    def solve(h):
        k_rows[:, h * d : (h + 1) * d] = k_ref[:, :, h * d : (h + 1) * d].reshape(steps, d)
        v_rows[:, h * d : (h + 1) * d] = v_ref[:, :, h * d : (h + 1) * d].reshape(steps, d)
        k = k_rows[:, h * d : (h + 1) * d]
        kf = k.astype(f32)
        sq = split2(kf * kf)
        yield
        n_c = lax.rsqrt(sum(mm(p, onesd) for p in sq) + eps_norm)
        n_r = lax.rsqrt(sum(nt(ones8, p) for p in sq) + eps_norm)[:1]
        nrow[h] = n_r
        c_h = jnp.broadcast_to(c_col[:, h : h + 1], (steps, d))
        row = c_row[h : h + 1, :]
        yield

        def coupled(i, j):
            at, to = slice(i * half, (i + 1) * half), slice(j * half, (j + 1) * half)
            gap = jnp.minimum(c_h[at] - row[:, to], 0.0)
            return jnp.exp(gap) * nt(k[at], k[to]) * (2.0 * n_r[:, to]) * n_c[at]

        diag = [jnp.where(below, coupled(i, i), 0.0) for i in range(2)]
        joint = coupled(1, 0)
        yield
        tri = [wide(x) for x in diag]
        invs = [eye - jnp.where(close, x, 0.0) for x in diag]
        wides = [wide(x) for x in invs]
        yield
        for b in levels:
            spans = [(i, i + b) for i in range(0, half, b)]

            def odd(x):
                return jnp.concatenate([x[p:q] for p, q in spans[1::2]], axis=0)

            def mixed(x, new):
                return jnp.concatenate(
                    [x[p:q] if n % 2 == 0 else new[(n // 2) * b : (n // 2 + 1) * b] for n, (p, q) in enumerate(spans)],
                    axis=0,
                )

            olds = invs if b < 8 else [odd(x) for x in invs]
            if b < 8:
                rows = wides
            elif b < 16:
                rows = [wide(x) for x in olds]
            else:
                rows = [odd(x) for x in wides]
            ts = [mm4(rows[i], twice(tri[i] * keeps[b]), half) for i in range(2)]
            yield
            ts = [wide(t) for t in ts]
            news = [olds[i] - mm4(ts[i], twice(wides[i]), half) for i in range(2)]
            yield
            if b < 8:
                invs = news
                wides = [wide(x) for x in invs]
            else:
                invs = [mixed(x, new) for x, new in zip(invs, news)]
                if b < 16:
                    wides = [wide(x) for x in invs]
                else:
                    wides = [mixed(x, wide(new)) for x, new in zip(wides, news)]
        first, second = wides
        t = mm4(second, square(joint), half)
        k = k_rows[:, h * d : (h + 1) * d].astype(f32)
        v = v_rows[:, h * d : (h + 1) * d]
        yield
        rhs = jnp.concatenate([v, wide(jnp.exp(c_h) * n_c * k)], axis=1)
        across = wide(-mm4(wide(t), twice(first), half))
        top = mm(first, twice(rhs[:half]))
        yield
        low = mm(jnp.concatenate([across, second], axis=1),
                 jnp.concatenate([twice(rhs[:half]), twice(rhs[half:])], axis=0))
        last = c_col[steps - 1 :, h : h + 1]
        tail = jnp.exp(c_h[steps - 1 :] - c_h) * (2.0 * n_c)
        t_hi, t_lo = split2(jnp.transpose(tail * k))
        yield
        x = jnp.concatenate([top, low], axis=0)
        x_hi, x_lo = split2(jnp.concatenate([x[:, :d], x[:, d : 2 * d] + x[:, 2 * d :]], axis=1))
        solved[h] = (x_hi, x_lo)
        yield
        ba = mm(t_hi, x_hi) + mm(t_lo, x_hi) + mm(t_hi, x_lo)
        yield
        ba = jnp.transpose(ba)
        maps[h] = jnp.concatenate([jnp.exp(last) * eye_d - ba[d:], ba[:d]], axis=0)

    def inside(h):
        k = k_rows[:, h * d : (h + 1) * d]
        x_hi, x_lo = solved[h]
        q = q_ref[:, h * d : (h + 1) * d]
        qc = q_col[:, h : h + 1]
        qgap = jnp.minimum(qc - c_row[h : h + 1, :], 0.0)
        pairs = jnp.where(visible, jnp.exp(qgap) * nt(q, k) * (2.0 * nrow[h]), 0.0)
        yield
        p_hi, p_lo = split2(pairs)
        px = mm(p_hi, x_hi) + mm(p_lo, x_hi) + mm(p_hi, x_lo)
        yield
        lo_ref[h] = px[:, :d]
        r_ref[h] = wide(jnp.exp(qc) * q.astype(f32) - px[:, d:])

    def together(works, after=None, step=0):
        works = list(works)
        rounds = 0
        while works:
            works = [work for work in works if next(work, works) is not works]
            rounds += 1
            if after is not None and rounds == step:
                after()

    early = me < inner

    def send(j, mine):
        @pl.when(mine)
        def _():
            for k in (2, 0, 1):
                map_copy(j, k).start()

    late = jnp.logical_not(early)
    for j in range(own):
        hs = range(4 * j, 4 * j + 4)
        for h in hs:
            fetch(h, 0).wait()
            fetch(h, 1).wait()
        together((solve(h) for h in hs), )
        if j == 0:
            greeted()
        send(j, early)
        if j < own - 1:
            send(j, late)

    if not direct:
        send(own - 1, late)
    for copy in others[1:]:
        copy.wait()
    for j in range(own):
        together(inside(h) for h in range(4 * j, 4 * j + 4))
    if direct:
        @pl.when(early)
        def _():
            for k in (2,):
                map_copy(own - 1, k).wait_send()
            pl.semaphore_signal(turn_sem, inc=1, device_id=place(me + 8), device_id_type=MESH)

        @pl.when(late)
        def _():
            pl.semaphore_wait(turn_sem, 1)

        send(own - 1, late)


    def add_low(both, low):
        return jnp.concatenate([both[:d], both[d:] + low], axis=0)

    def compose(j):
        gath[pos, j] = maps[4 * j + pos]
        for k in range(3):
            map_from(j, k).wait_recv()
        m = [gath[i, j] for i in range(4)]
        second = square(m[1][:d])
        third = square(m[2][:d])
        m01 = add_low(mm4(wide(m[0]), second, d), m[1][d:])
        m23 = add_low(mm4(wide(m[2]), square(m[3][:d]), d), m[3][d:])
        w01 = wide(m01)
        whole = add_low(mm4(w01, square(m23[:d]), d), m23[d:])
        total[j] = whole

        if direct:
            @pl.when(quad == 0)
            def _():
                x_copy(j, total.at[j, pl.ds(d, d)], 1).start()
                x_copy(j, total.at[j, pl.ds(d, d)], 2).start()

            @pl.when((quad == 1) | (quad == 2))
            def _():
                y_copy(j).start()

        m012 = add_low(mm4(w01, third, d), m[2][d:])
        for i, x in enumerate((m[0], m01, m012)):
            pre_sq[j, i] = square(x[:d])
            pre[j, i] = x[d:]

    def give(j, start):
        starts[j, 0] = start
        rows = wide(start)
        for i in range(3):
            starts[j, i + 1] = mm4(rows, pre_sq[j, i], d) + pre[j, i]
        for k in (2, 0, 1):
            back_copy(j, k).start()

    def pass_on(j, start, hop):
        x_out[j] = mm4(wide(start), square(total[j, :d]), d) + total[j, d:]
        x_copy(j, x_out.at[j], hop).start()

    for j in range(own):
        compose(j)

        @pl.when(quad == 0)
        def _():
            if not direct:
                x_copy(j, total.at[j, pl.ds(d, d)], 1).start()
            give(j, jnp.zeros((d, d), f32))

    for j in range(own):
        if direct:
            @pl.when(quad == 1)
            def _():
                x_copy(j, x_out.at[j], 1).wait_recv()
                pass_on(j, x_in[j], 2)
                give(j, x_in[j])

            @pl.when(quad >= 2)
            def _():
                y_copy(j).wait_recv()
                x_copy(j, x_out.at[j], 1).wait_recv()
                give(j, mm4(wide(x_in[j]), square(y_in[j, :d]), d) + y_in[j, d:])
        else:
            @pl.when(quad >= 1)
            def _():
                x_copy(j, x_out.at[j], 1).wait_recv()

                @pl.when(quad < quads - 1)
                def _():
                    pass_on(j, x_in[j], 1)

                give(j, x_in[j])

    gain = gain_ref[...]

    def readout(h, state_t):
        both = nt(r_ref[h], square_t(state_t))
        out = both[:, :d] + both[:, d:] + lo_ref[h]
        scale = lax.rsqrt(jnp.mean(out * out, axis=-1, keepdims=True) + eps_norm)
        cols = pl.ds(pl.multiple_of(h * d, d), d)
        g = gate_ref[:, cols].astype(f32)
        o_ref[:, cols] = (out * scale * gain * (g / (1.0 + jnp.exp(-g)))).astype(bf16)

    for j in range(own):
        for k in range(3):
            @pl.when(late | (j < own - 1) | (not direct) | (k not in (2,)))
            def _():
                map_copy(j, k).wait_send()

    for j in range(own):
        readout(4 * j + pos, starts[j, pos])
        for k in range(3):
            back_copy(j, k).wait_recv()
            readout(4 * j + places[k], states[4 * j + places[k]])

    for j in range(own):
        for k in range(3):
            back_copy(j, k).wait_send()
        if direct:
            @pl.when(quad == 0)
            def _():
                x_copy(j, total.at[j, pl.ds(d, d)], 1).wait_send()

            @pl.when(quad < 2)
            def _():
                x_copy(j, x_out.at[j], 2).wait_send()

            @pl.when((quad == 1) | (quad == 2))
            def _():
                y_copy(j).wait_send()
        else:
            @pl.when(quad < quads - 1)
            def _():
                x_copy(j, x_out.at[j], 1).wait_send()


def solution(mesh):
    inner = mesh.shape["inner"]
    count = inner * mesh.shape["outer"]
    assert count % 4 == 0

    def local(queries, keys, values, log_gate, out_gate, norm_gain):
        toks, width = queries.shape
        heads = log_gate.shape[1]
        d = width // heads
        own = heads // 4
        dma = pltpu.SemaphoreType.DMA
        return pl.pallas_call(
            lambda *refs: kernel(inner, count, *refs),
            out_shape=jax.ShapeDtypeStruct((toks, width), bf16),
            in_specs=[pl.BlockSpec(memory_space=pltpu.HBM)] * 6,
            out_specs=pl.BlockSpec(memory_space=pltpu.VMEM),
            scratch_shapes=[
                pltpu.VMEM((toks, 2, width), bf16),
                pltpu.VMEM((toks, 2, width), bf16),
                pltpu.VMEM((2 * toks, width), bf16),
                pltpu.VMEM((2 * toks, width), bf16),
                pltpu.VMEM((toks, width), bf16),
                pltpu.VMEM((heads, toks), f32),
                pltpu.VMEM((toks, width), bf16),
                pltpu.VMEM((1, d), f32),
                dma((2 * heads + 4,)),
                pltpu.VMEM((heads, 2 * d, d), f32),
                pltpu.VMEM((4, own, 2 * d, d), f32),
                pltpu.VMEM((own, 3, d, d), f32),
                pltpu.VMEM((own, 3, 2 * d, 2 * d), bf16),
                pltpu.VMEM((own, 2 * d, d), f32),
                pltpu.VMEM((heads, d, 2 * d), bf16),
                pltpu.VMEM((heads, d, d), f32),
                pltpu.VMEM((own, d, d), f32),
                pltpu.VMEM((own, 2 * d, d), f32),
                pltpu.VMEM((own, d, d), f32),
                pltpu.VMEM((own, 4, d, d), f32),
                pltpu.VMEM((heads, d, d), f32),
                dma((heads,)), dma((own, 4)), dma((own, 2)), dma((own,)),
                dma((own,)), dma((own,)), dma((own, 3)), dma((own, 3)),
                pltpu.SemaphoreType.REGULAR,
            ],
            compiler_params=pltpu.CompilerParams(
                collective_id=0, has_side_effects=True, vmem_limit_bytes=48 << 20
            ),
            name="delta_product",
        )(*[pltpu.with_memory_space_constraint(x, pltpu.HBM) for x in (keys, values, queries, log_gate.T, out_gate, norm_gain.reshape(1, d))])

    spec = P(("groups", "outer", "inner"), None)
    spec3 = P(("groups", "outer", "inner"), None, None)
    return jax.shard_map(
        local, mesh=mesh, in_specs=(spec, spec3, spec3, spec, spec, P()), out_specs=spec, check_vma=False
    )
```

```python
import jax
import jax.numpy as jnp
from jax import lax
from jax.experimental import pallas as pl
from jax.experimental.pallas import tpu as pltpu
from jax.sharding import PartitionSpec as P

eps_norm = 1e-06
f32 = jnp.float32
bf16 = jnp.bfloat16
MESH = pl.DeviceIdType.MESH
NT = (((1,), (1,)), ((), ()))
TN = (((0,), (0,)), ((), ()))


def mm(a, b):
    return jnp.dot(a, b, preferred_element_type=f32)


def split2(x):
    hi = x.astype(bf16)
    return hi, (x - hi.astype(f32)).astype(bf16)


def split3(x):
    hi, rest = x.astype(bf16), None
    rest = x - hi.astype(f32)
    mid = rest.astype(bf16)
    return hi, mid, (rest - mid.astype(f32)).astype(bf16)


def wide(x):
    return jnp.concatenate(split2(x), axis=1)


def square(x):
    row = jnp.concatenate(split2(x), axis=1)
    return jnp.concatenate([row, row], axis=0)


def mm4(a_wide, b_square, size):
    both = mm(a_wide, b_square)
    return both[:, :size] + both[:, size:]


def twice(x):
    return jnp.concatenate([x, x], axis=0)


def square_t(x):
    hi, lo = split2(x)
    return jnp.concatenate(
        [jnp.concatenate([hi, hi], axis=1), jnp.concatenate([lo, lo], axis=1)], axis=0
    )


def iotas(r, c):
    return (
        lax.broadcasted_iota(jnp.int32, (r, c), 0),
        lax.broadcasted_iota(jnp.int32, (r, c), 1),
    )


def nt(a, b):
    return lax.dot_general(a, b, NT, preferred_element_type=f32)


def kernel(inner, count, k_hbm, v_hbm, q_hbm, lg_hbm, gate_hbm, gain_hbm, o_ref,
           k_ref, v_ref, k_rows, v_rows, q_ref, lg_ref, gate_ref, gain_ref, in_sems, maps, gath, pre, pre_sq, total, r_ref, lo_ref, x_in, y_in, x_out, starts, states,
           map_send, map_recv, x_send, x_recv, y_send, y_recv, back_send, back_recv, turn_sem):
    toks, width = q_ref.shape
    steps = 2 * toks
    heads = lg_ref.shape[0]
    d = width // heads
    half = steps // 2
    own = heads // 4
    quads = count // 4
    direct = quads == 4

    me = lax.axis_index("outer") * inner + lax.axis_index("inner")
    pos = me % 4
    quad = me // 4
    places = [pos + 1 - 2 * (pos % 2), pos + 2 - 4 * (pos // 2), 3 - pos]

    def place(i):
        return {"outer": i // inner, "inner": i % inner}

    barrier = pltpu.get_barrier_semaphore()

    def greet(i):
        pl.semaphore_signal(barrier, inc=1, device_id=place(i), device_id_type=MESH)

    for at in places:
        greet(4 * quad + at)

    @pl.when(quad >= 1)
    def _():
        greet(me - 4)

    if direct:
        @pl.when(quad >= 2)
        def _():
            greet(me - 8)

    def greeted():
        hops = 2 if direct else 1

        for more in range(hops + 1):
            @pl.when((quad < quads - hops) if more == hops else (quad == quads - 1 - more))
            def _():
                pl.semaphore_wait(barrier, 3 + more)

    def remote(src, dst, send, recv, target):
        return pltpu.make_async_remote_copy(
            src_ref=src, dst_ref=dst, send_sem=send, recv_sem=recv,
            device_id=place(target), device_id_type=MESH,
        )

    def map_copy(j, k):
        h = 4 * j + places[k]
        return remote(maps.at[h], gath.at[pos, j], map_send.at[h], map_recv.at[j, pos], 4 * quad + places[k])

    def map_from(j, k):
        return remote(maps.at[0], gath.at[places[k], j], map_send.at[0], map_recv.at[j, places[k]],
                      4 * quad + places[k])

    def back_copy(j, k):
        return remote(starts.at[j, places[k]], states.at[4 * j + pos], back_send.at[j, k], back_recv.at[j, k],
                      4 * quad + places[k])

    def x_copy(j, src, hop):
        return remote(src, x_in.at[j], x_send.at[j, hop - 1], x_recv.at[j], me + 4 * hop)

    def y_copy(j):
        return remote(total.at[j], y_in.at[j], y_send.at[j], y_recv.at[j], me + 4)

    def fetch(h, which):
        src, dst = ((k_hbm, k_ref), (v_hbm, v_ref))[which]
        cols = pl.ds(h * d, d)
        return pltpu.make_async_copy(src.at[:, :, cols], dst.at[:, :, cols], in_sems.at[2 * h + which])

    others = [
        pltpu.make_async_copy(src, dst, in_sems.at[2 * heads + i])
        for i, (src, dst) in enumerate(
            ((lg_hbm, lg_ref), (q_hbm, q_ref), (gate_hbm, gate_ref), (gain_hbm, gain_ref))
        )
    ]
    others[0].start()
    for h in range(heads):
        fetch(h, 0).start()
        fetch(h, 1).start()
    for copy in others[1:]:
        copy.start()

    i_st, j_tk = iotas(steps, toks)
    tri_steps = (j_tk <= i_st // 2).astype(f32).astype(bf16)
    i_tk, j_tk2 = iotas(toks, toks)
    tri_toks = (j_tk2 <= i_tk).astype(f32).astype(bf16)
    others[0].wait()
    lgs = split3(lg_ref[...])
    c_col = sum(nt(tri_steps, p) for p in lgs)
    q_col = sum(nt(tri_toks, p) for p in lgs)
    c_row = sum(nt(p, tri_steps) for p in lgs)
    it, jt = iotas(toks, steps)
    visible = jt <= 2 * it + 1
    hi_, hj_ = iotas(half, half)
    eye = (hi_ == hj_).astype(f32)
    di, dj = iotas(d, d)
    levels = [2**i for i in range(1, half.bit_length() - 1)]
    corner = {
        b: ((hi_ // (2 * b) == hj_ // (2 * b)) & ((hi_ // b) % 2 == 1) & ((hj_ // b) % 2 == 0)).astype(f32).astype(bf16)
        for b in levels
    }
    below = hi_ > hj_
    close = hi_ // 2 == hj_ // 2
    eye_d = (di == dj).astype(f32)
    ones8 = jnp.ones((8, d), bf16)
    onesd = jnp.ones((d, d), bf16)

    nrow, solved = {}, {}
    keeps = {b: jnp.concatenate([corner[b]] * 2, axis=1) for b in levels}

    def solve(h):
        k_rows[:, h * d : (h + 1) * d] = k_ref[:, :, h * d : (h + 1) * d].reshape(steps, d)
        v_rows[:, h * d : (h + 1) * d] = v_ref[:, :, h * d : (h + 1) * d].reshape(steps, d)
        k = k_rows[:, h * d : (h + 1) * d]
        kf = k.astype(f32)
        sq = split2(kf * kf)
        yield
        n_c = lax.rsqrt(sum(mm(p, onesd) for p in sq) + eps_norm)
        n_r = lax.rsqrt(sum(nt(ones8, p) for p in sq) + eps_norm)[:1]
        nrow[h] = n_r
        c_h = jnp.broadcast_to(c_col[:, h : h + 1], (steps, d))
        row = c_row[h : h + 1, :]
        yield

        def coupled(i, j):
            at, to = slice(i * half, (i + 1) * half), slice(j * half, (j + 1) * half)
            gap = jnp.minimum(c_h[at] - row[:, to], 0.0)
            return jnp.exp(gap) * nt(k[at], k[to]) * (2.0 * n_r[:, to]) * n_c[at]

        diag = [jnp.where(below, coupled(i, i), 0.0) for i in range(2)]
        joint = coupled(1, 0)
        yield
        tri = [wide(x) for x in diag]
        invs = [eye - jnp.where(close, x, 0.0) for x in diag]
        wides = [wide(x) for x in invs]
        yield
        for b in levels:
            spans = [(i, i + b) for i in range(0, half, b)]

            def odd(x):
                return jnp.concatenate([x[p:q] for p, q in spans[1::2]], axis=0)

            def mixed(x, new):
                return jnp.concatenate(
                    [x[p:q] if n % 2 == 0 else new[(n // 2) * b : (n // 2 + 1) * b] for n, (p, q) in enumerate(spans)],
                    axis=0,
                )

            olds = invs if b < 8 else [odd(x) for x in invs]
            if b < 8:
                rows = wides
            elif b < 16:
                rows = [wide(x) for x in olds]
            else:
                rows = [odd(x) for x in wides]
            ts = [mm4(rows[i], twice(tri[i] * keeps[b]), half) for i in range(2)]
            yield
            ts = [wide(t) for t in ts]
            news = [olds[i] - mm4(ts[i], twice(wides[i]), half) for i in range(2)]
            yield
            if b < 8:
                invs = news
                wides = [wide(x) for x in invs]
            else:
                invs = [mixed(x, new) for x, new in zip(invs, news)]
                if b < 16:
                    wides = [wide(x) for x in invs]
                else:
                    wides = [mixed(x, wide(new)) for x, new in zip(wides, news)]
        first, second = wides
        t = mm4(second, square(joint), half)
        k = k_rows[:, h * d : (h + 1) * d].astype(f32)
        v = v_rows[:, h * d : (h + 1) * d]
        yield
        rhs = jnp.concatenate([v, wide(jnp.exp(c_h) * n_c * k)], axis=1)
        across = wide(-mm4(wide(t), twice(first), half))
        top = mm(first, twice(rhs[:half]))
        yield
        low = mm(jnp.concatenate([across, second], axis=1),
                 jnp.concatenate([twice(rhs[:half]), twice(rhs[half:])], axis=0))
        last = c_col[steps - 1 :, h : h + 1]
        tail = jnp.exp(c_h[steps - 1 :] - c_h) * (2.0 * n_c)
        t_hi, t_lo = split2(jnp.transpose(tail * k))
        yield
        x = jnp.concatenate([top, low], axis=0)
        x_hi, x_lo = split2(jnp.concatenate([x[:, :d], x[:, d : 2 * d] + x[:, 2 * d :]], axis=1))
        solved[h] = (x_hi, x_lo)
        yield
        ba = mm(t_hi, x_hi) + mm(t_lo, x_hi) + mm(t_hi, x_lo)
        yield
        ba = jnp.transpose(ba)
        maps[h] = jnp.concatenate([jnp.exp(last) * eye_d - ba[d:], ba[:d]], axis=0)

    def inside(h):
        k = k_rows[:, h * d : (h + 1) * d]
        x_hi, x_lo = solved[h]
        q = q_ref[:, h * d : (h + 1) * d]
        qc = q_col[:, h : h + 1]
        qgap = jnp.minimum(qc - c_row[h : h + 1, :], 0.0)
        pairs = jnp.where(visible, jnp.exp(qgap) * nt(q, k) * (2.0 * nrow[h]), 0.0)
        yield
        p_hi, p_lo = split2(pairs)
        px = mm(p_hi, x_hi) + mm(p_lo, x_hi) + mm(p_hi, x_lo)
        yield
        lo_ref[h] = px[:, :d]
        r_ref[h] = wide(jnp.exp(qc) * q.astype(f32) - px[:, d:])

    def together(works, after=None, step=0):
        works = list(works)
        rounds = 0
        while works:
            works = [work for work in works if next(work, works) is not works]
            rounds += 1
            if after is not None and rounds == step:
                after()

    early = me < inner

    def send(j, mine):
        @pl.when(mine)
        def _():
            for k in (2, 0, 1):
                map_copy(j, k).start()

    late = jnp.logical_not(early)
    for j in range(own):
        hs = range(4 * j, 4 * j + 4)
        for h in hs:
            fetch(h, 0).wait()
            fetch(h, 1).wait()
        together((solve(h) for h in hs), )
        if j == 0:
            greeted()
        send(j, early)
        if j < own - 1:
            send(j, late)

    if not direct:
        send(own - 1, late)
    for copy in others[1:]:
        copy.wait()
    for j in range(own):
        together(inside(h) for h in range(4 * j, 4 * j + 4))
    if direct:
        @pl.when(early)
        def _():
            for k in (2,):
                map_copy(own - 1, k).wait_send()
            pl.semaphore_signal(turn_sem, inc=1, device_id=place(me + 8), device_id_type=MESH)

        @pl.when(late)
        def _():
            for k in (0, 1):
                map_copy(own - 1, k).start()
            pl.semaphore_wait(turn_sem, 1)
            for k in (2,):
                map_copy(own - 1, k).start()


    def add_low(both, low):
        return jnp.concatenate([both[:d], both[d:] + low], axis=0)

    def compose(j):
        gath[pos, j] = maps[4 * j + pos]
        for k in range(3):
            map_from(j, k).wait_recv()
        m = [gath[i, j] for i in range(4)]
        second = square(m[1][:d])
        third = square(m[2][:d])
        m01 = add_low(mm4(wide(m[0]), second, d), m[1][d:])
        m23 = add_low(mm4(wide(m[2]), square(m[3][:d]), d), m[3][d:])
        w01 = wide(m01)
        whole = add_low(mm4(w01, square(m23[:d]), d), m23[d:])
        total[j] = whole

        if direct:
            @pl.when(quad == 0)
            def _():
                x_copy(j, total.at[j, pl.ds(d, d)], 1).start()
                x_copy(j, total.at[j, pl.ds(d, d)], 2).start()

            @pl.when((quad == 1) | (quad == 2))
            def _():
                y_copy(j).start()

        m012 = add_low(mm4(w01, third, d), m[2][d:])
        for i, x in enumerate((m[0], m01, m012)):
            pre_sq[j, i] = square(x[:d])
            pre[j, i] = x[d:]

    def give(j, start):
        starts[j, 0] = start
        rows = wide(start)
        for i in range(3):
            starts[j, i + 1] = mm4(rows, pre_sq[j, i], d) + pre[j, i]
        for k in (2, 0, 1):
            back_copy(j, k).start()

    def pass_on(j, start, hop):
        x_out[j] = mm4(wide(start), square(total[j, :d]), d) + total[j, d:]
        x_copy(j, x_out.at[j], hop).start()

    for j in range(own):
        compose(j)

        @pl.when(quad == 0)
        def _():
            if not direct:
                x_copy(j, total.at[j, pl.ds(d, d)], 1).start()
            give(j, jnp.zeros((d, d), f32))

    for j in range(own):
        if direct:
            @pl.when(quad == 1)
            def _():
                x_copy(j, x_out.at[j], 1).wait_recv()
                pass_on(j, x_in[j], 2)
                give(j, x_in[j])

            @pl.when(quad >= 2)
            def _():
                y_copy(j).wait_recv()
                x_copy(j, x_out.at[j], 1).wait_recv()
                give(j, mm4(wide(x_in[j]), square(y_in[j, :d]), d) + y_in[j, d:])
        else:
            @pl.when(quad >= 1)
            def _():
                x_copy(j, x_out.at[j], 1).wait_recv()

                @pl.when(quad < quads - 1)
                def _():
                    pass_on(j, x_in[j], 1)

                give(j, x_in[j])

    gain = gain_ref[...]

    def readout(h, state_t):
        both = nt(r_ref[h], square_t(state_t))
        out = both[:, :d] + both[:, d:] + lo_ref[h]
        scale = lax.rsqrt(jnp.mean(out * out, axis=-1, keepdims=True) + eps_norm)
        cols = pl.ds(pl.multiple_of(h * d, d), d)
        g = gate_ref[:, cols].astype(f32)
        o_ref[:, cols] = (out * scale * gain * (g / (1.0 + jnp.exp(-g)))).astype(bf16)

    for j in range(own):
        for k in range(3):
            @pl.when(late | (j < own - 1) | (not direct) | (k not in (2,)))
            def _():
                map_copy(j, k).wait_send()

    for j in range(own):
        readout(4 * j + pos, starts[j, pos])
        for k in range(3):
            back_copy(j, k).wait_recv()
            readout(4 * j + places[k], states[4 * j + places[k]])

    for j in range(own):
        for k in range(3):
            back_copy(j, k).wait_send()
        if direct:
            @pl.when(quad == 0)
            def _():
                x_copy(j, total.at[j, pl.ds(d, d)], 1).wait_send()

            @pl.when(quad < 2)
            def _():
                x_copy(j, x_out.at[j], 2).wait_send()

            @pl.when((quad == 1) | (quad == 2))
            def _():
                y_copy(j).wait_send()
        else:
            @pl.when(quad < quads - 1)
            def _():
                x_copy(j, x_out.at[j], 1).wait_send()


def solution(mesh):
    inner = mesh.shape["inner"]
    count = inner * mesh.shape["outer"]
    assert count % 4 == 0

    def local(queries, keys, values, log_gate, out_gate, norm_gain):
        toks, width = queries.shape
        heads = log_gate.shape[1]
        d = width // heads
        own = heads // 4
        dma = pltpu.SemaphoreType.DMA
        return pl.pallas_call(
            lambda *refs: kernel(inner, count, *refs),
            out_shape=jax.ShapeDtypeStruct((toks, width), bf16),
            in_specs=[pl.BlockSpec(memory_space=pltpu.HBM)] * 6,
            out_specs=pl.BlockSpec(memory_space=pltpu.VMEM),
            scratch_shapes=[
                pltpu.VMEM((toks, 2, width), bf16),
                pltpu.VMEM((toks, 2, width), bf16),
                pltpu.VMEM((2 * toks, width), bf16),
                pltpu.VMEM((2 * toks, width), bf16),
                pltpu.VMEM((toks, width), bf16),
                pltpu.VMEM((heads, toks), f32),
                pltpu.VMEM((toks, width), bf16),
                pltpu.VMEM((1, d), f32),
                dma((2 * heads + 4,)),
                pltpu.VMEM((heads, 2 * d, d), f32),
                pltpu.VMEM((4, own, 2 * d, d), f32),
                pltpu.VMEM((own, 3, d, d), f32),
                pltpu.VMEM((own, 3, 2 * d, 2 * d), bf16),
                pltpu.VMEM((own, 2 * d, d), f32),
                pltpu.VMEM((heads, d, 2 * d), bf16),
                pltpu.VMEM((heads, d, d), f32),
                pltpu.VMEM((own, d, d), f32),
                pltpu.VMEM((own, 2 * d, d), f32),
                pltpu.VMEM((own, d, d), f32),
                pltpu.VMEM((own, 4, d, d), f32),
                pltpu.VMEM((heads, d, d), f32),
                dma((heads,)), dma((own, 4)), dma((own, 2)), dma((own,)),
                dma((own,)), dma((own,)), dma((own, 3)), dma((own, 3)),
                pltpu.SemaphoreType.REGULAR,
            ],
            compiler_params=pltpu.CompilerParams(
                collective_id=0, has_side_effects=True, vmem_limit_bytes=48 << 20
            ),
            name="delta_product",
        )(*[pltpu.with_memory_space_constraint(x, pltpu.HBM) for x in (keys, values, queries, log_gate.T, out_gate, norm_gain.reshape(1, d))])

    spec = P(("groups", "outer", "inner"), None)
    spec3 = P(("groups", "outer", "inner"), None, None)
    return jax.shard_map(
        local, mesh=mesh, in_specs=(spec, spec3, spec3, spec, spec, P()), out_specs=spec, check_vma=False
    )
```

```python
import jax
import jax.numpy as jnp
from jax import lax
from jax.experimental import pallas as pl
from jax.experimental.pallas import tpu as pltpu
from jax.sharding import PartitionSpec as P

eps_norm = 1e-06
f32 = jnp.float32
bf16 = jnp.bfloat16
MESH = pl.DeviceIdType.MESH
NT = (((1,), (1,)), ((), ()))
TN = (((0,), (0,)), ((), ()))


def mm(a, b):
    return jnp.dot(a, b, preferred_element_type=f32)


def split2(x):
    hi = x.astype(bf16)
    return hi, (x - hi.astype(f32)).astype(bf16)


def split3(x):
    hi, rest = x.astype(bf16), None
    rest = x - hi.astype(f32)
    mid = rest.astype(bf16)
    return hi, mid, (rest - mid.astype(f32)).astype(bf16)


def wide(x):
    return jnp.concatenate(split2(x), axis=1)


def square(x):
    row = jnp.concatenate(split2(x), axis=1)
    return jnp.concatenate([row, row], axis=0)


def mm4(a_wide, b_square, size):
    both = mm(a_wide, b_square)
    return both[:, :size] + both[:, size:]


def twice(x):
    return jnp.concatenate([x, x], axis=0)


def square_t(x):
    hi, lo = split2(x)
    return jnp.concatenate(
        [jnp.concatenate([hi, hi], axis=1), jnp.concatenate([lo, lo], axis=1)], axis=0
    )


def iotas(r, c):
    return (
        lax.broadcasted_iota(jnp.int32, (r, c), 0),
        lax.broadcasted_iota(jnp.int32, (r, c), 1),
    )


def nt(a, b):
    return lax.dot_general(a, b, NT, preferred_element_type=f32)


def kernel(inner, count, k_hbm, v_hbm, q_hbm, lg_hbm, gate_hbm, gain_hbm, o_ref,
           k_ref, v_ref, k_rows, v_rows, q_ref, lg_ref, gate_ref, gain_ref, in_sems, maps, gath, pre, pre_sq, total, r_ref, lo_ref, x_in, y_in, x_out, starts, states,
           map_send, map_recv, x_send, x_recv, y_send, y_recv, back_send, back_recv, turn_sem):
    toks, width = q_ref.shape
    steps = 2 * toks
    heads = lg_ref.shape[0]
    d = width // heads
    half = steps // 2
    own = heads // 4
    quads = count // 4
    direct = quads == 4

    me = lax.axis_index("outer") * inner + lax.axis_index("inner")
    pos = me % 4
    quad = me // 4
    places = [pos + 1 - 2 * (pos % 2), pos + 2 - 4 * (pos // 2), 3 - pos]

    def place(i):
        return {"outer": i // inner, "inner": i % inner}

    barrier = pltpu.get_barrier_semaphore()

    def greet(i):
        pl.semaphore_signal(barrier, inc=1, device_id=place(i), device_id_type=MESH)

    for at in places:
        greet(4 * quad + at)

    @pl.when(quad >= 1)
    def _():
        greet(me - 4)

    if direct:
        @pl.when(quad >= 2)
        def _():
            greet(me - 8)

    def greeted():
        hops = 2 if direct else 1

        for more in range(hops + 1):
            @pl.when((quad < quads - hops) if more == hops else (quad == quads - 1 - more))
            def _():
                pl.semaphore_wait(barrier, 3 + more)

    def remote(src, dst, send, recv, target):
        return pltpu.make_async_remote_copy(
            src_ref=src, dst_ref=dst, send_sem=send, recv_sem=recv,
            device_id=place(target), device_id_type=MESH,
        )

    def map_copy(j, k):
        h = 4 * j + places[k]
        return remote(maps.at[h], gath.at[pos, j], map_send.at[h], map_recv.at[j, pos], 4 * quad + places[k])

    def map_from(j, k):
        return remote(maps.at[0], gath.at[places[k], j], map_send.at[0], map_recv.at[j, places[k]],
                      4 * quad + places[k])

    def back_copy(j, k):
        return remote(starts.at[j, places[k]], states.at[4 * j + pos], back_send.at[j, k], back_recv.at[j, k],
                      4 * quad + places[k])

    def x_copy(j, src, hop):
        return remote(src, x_in.at[j], x_send.at[j, hop - 1], x_recv.at[j], me + 4 * hop)

    def y_copy(j):
        return remote(total.at[j], y_in.at[j], y_send.at[j], y_recv.at[j], me + 4)

    def fetch(h, which):
        src, dst = ((k_hbm, k_ref), (v_hbm, v_ref))[which]
        cols = pl.ds(h * d, d)
        return pltpu.make_async_copy(src.at[:, :, cols], dst.at[:, :, cols], in_sems.at[2 * h + which])

    others = [
        pltpu.make_async_copy(src, dst, in_sems.at[2 * heads + i])
        for i, (src, dst) in enumerate(
            ((lg_hbm, lg_ref), (q_hbm, q_ref), (gate_hbm, gate_ref), (gain_hbm, gain_ref))
        )
    ]
    others[0].start()
    for h in range(heads):
        fetch(h, 0).start()
        fetch(h, 1).start()
    for copy in others[1:]:
        copy.start()

    i_st, j_tk = iotas(steps, toks)
    tri_steps = (j_tk <= i_st // 2).astype(f32).astype(bf16)
    i_tk, j_tk2 = iotas(toks, toks)
    tri_toks = (j_tk2 <= i_tk).astype(f32).astype(bf16)
    others[0].wait()
    lgs = split3(lg_ref[...])
    c_col = sum(nt(tri_steps, p) for p in lgs)
    q_col = sum(nt(tri_toks, p) for p in lgs)
    c_row = sum(nt(p, tri_steps) for p in lgs)
    it, jt = iotas(toks, steps)
    visible = jt <= 2 * it + 1
    hi_, hj_ = iotas(half, half)
    eye = (hi_ == hj_).astype(f32)
    di, dj = iotas(d, d)
    levels = [2**i for i in range(1, half.bit_length() - 1)]
    corner = {
        b: ((hi_ // (2 * b) == hj_ // (2 * b)) & ((hi_ // b) % 2 == 1) & ((hj_ // b) % 2 == 0)).astype(f32).astype(bf16)
        for b in levels
    }
    below = hi_ > hj_
    close = hi_ // 2 == hj_ // 2
    eye_d = (di == dj).astype(f32)
    ones8 = jnp.ones((8, d), bf16)
    onesd = jnp.ones((d, d), bf16)

    nrow, solved = {}, {}
    keeps = {b: jnp.concatenate([corner[b]] * 2, axis=1) for b in levels}

    def solve(h):
        k_rows[:, h * d : (h + 1) * d] = k_ref[:, :, h * d : (h + 1) * d].reshape(steps, d)
        v_rows[:, h * d : (h + 1) * d] = v_ref[:, :, h * d : (h + 1) * d].reshape(steps, d)
        k = k_rows[:, h * d : (h + 1) * d]
        kf = k.astype(f32)
        sq = split2(kf * kf)
        yield
        n_c = lax.rsqrt(sum(mm(p, onesd) for p in sq) + eps_norm)
        n_r = lax.rsqrt(sum(nt(ones8, p) for p in sq) + eps_norm)[:1]
        nrow[h] = n_r
        c_h = jnp.broadcast_to(c_col[:, h : h + 1], (steps, d))
        row = c_row[h : h + 1, :]
        yield

        def coupled(i, j):
            at, to = slice(i * half, (i + 1) * half), slice(j * half, (j + 1) * half)
            gap = jnp.minimum(c_h[at] - row[:, to], 0.0)
            return jnp.exp(gap) * nt(k[at], k[to]) * (2.0 * n_r[:, to]) * n_c[at]

        diag = [jnp.where(below, coupled(i, i), 0.0) for i in range(2)]
        joint = coupled(1, 0)
        yield
        tri = [wide(x) for x in diag]
        invs = [eye - jnp.where(close, x, 0.0) for x in diag]
        wides = [wide(x) for x in invs]
        yield
        for b in levels:
            spans = [(i, i + b) for i in range(0, half, b)]

            def odd(x):
                return jnp.concatenate([x[p:q] for p, q in spans[1::2]], axis=0)

            def mixed(x, new):
                return jnp.concatenate(
                    [x[p:q] if n % 2 == 0 else new[(n // 2) * b : (n // 2 + 1) * b] for n, (p, q) in enumerate(spans)],
                    axis=0,
                )

            olds = invs if b < 8 else [odd(x) for x in invs]
            if b < 8:
                rows = wides
            elif b < 16:
                rows = [wide(x) for x in olds]
            else:
                rows = [odd(x) for x in wides]
            ts = [mm4(rows[i], twice(tri[i] * keeps[b]), half) for i in range(2)]
            yield
            ts = [wide(t) for t in ts]
            news = [olds[i] - mm4(ts[i], twice(wides[i]), half) for i in range(2)]
            yield
            if b < 8:
                invs = news
                wides = [wide(x) for x in invs]
            else:
                invs = [mixed(x, new) for x, new in zip(invs, news)]
                if b < 16:
                    wides = [wide(x) for x in invs]
                else:
                    wides = [mixed(x, wide(new)) for x, new in zip(wides, news)]
        first, second = wides
        t = mm4(second, square(joint), half)
        k = k_rows[:, h * d : (h + 1) * d].astype(f32)
        v = v_rows[:, h * d : (h + 1) * d]
        yield
        rhs = jnp.concatenate([v, wide(jnp.exp(c_h) * n_c * k)], axis=1)
        across = wide(-mm4(wide(t), twice(first), half))
        top = mm(first, twice(rhs[:half]))
        yield
        low = mm(jnp.concatenate([across, second], axis=1),
                 jnp.concatenate([twice(rhs[:half]), twice(rhs[half:])], axis=0))
        last = c_col[steps - 1 :, h : h + 1]
        tail = jnp.exp(c_h[steps - 1 :] - c_h) * (2.0 * n_c)
        t_hi, t_lo = split2(jnp.transpose(tail * k))
        yield
        x = jnp.concatenate([top, low], axis=0)
        x_hi, x_lo = split2(jnp.concatenate([x[:, :d], x[:, d : 2 * d] + x[:, 2 * d :]], axis=1))
        solved[h] = (x_hi, x_lo)
        yield
        ba = mm(t_hi, x_hi) + mm(t_lo, x_hi) + mm(t_hi, x_lo)
        yield
        ba = jnp.transpose(ba)
        maps[h] = jnp.concatenate([jnp.exp(last) * eye_d - ba[d:], ba[:d]], axis=0)

    def inside(h):
        k = k_rows[:, h * d : (h + 1) * d]
        x_hi, x_lo = solved[h]
        q = q_ref[:, h * d : (h + 1) * d]
        qc = q_col[:, h : h + 1]
        qgap = jnp.minimum(qc - c_row[h : h + 1, :], 0.0)
        pairs = jnp.where(visible, jnp.exp(qgap) * nt(q, k) * (2.0 * nrow[h]), 0.0)
        yield
        p_hi, p_lo = split2(pairs)
        px = mm(p_hi, x_hi) + mm(p_lo, x_hi) + mm(p_hi, x_lo)
        yield
        lo_ref[h] = px[:, :d]
        r_ref[h] = wide(jnp.exp(qc) * q.astype(f32) - px[:, d:])

    def together(works, after=None, step=0):
        works = list(works)
        rounds = 0
        while works:
            works = [work for work in works if next(work, works) is not works]
            rounds += 1
            if after is not None and rounds == step:
                after()

    early = me < inner

    def send(j, mine, order=(2, 0, 1)):
        @pl.when(mine)
        def _():
            for k in order:
                map_copy(j, k).start()

    late = jnp.logical_not(early)
    for j in range(own):
        hs = range(4 * j, 4 * j + 4)
        for h in hs:
            fetch(h, 0).wait()
            fetch(h, 1).wait()
        together((solve(h) for h in hs), )
        if j == 0:
            greeted()
        send(j, early)
        if j < own - 1:
            send(j, late, (0, 1, 2))

    if direct:
        @pl.when(late)
        def _():
            for k in (0, 1):
                map_copy(own - 1, k).start()
    else:
        send(own - 1, late)
    for copy in others[1:]:
        copy.wait()
    for j in range(own):
        together(inside(h) for h in range(4 * j, 4 * j + 4))
    if direct:
        @pl.when(early)
        def _():
            for k in (2,):
                map_copy(own - 1, k).wait_send()
            pl.semaphore_signal(turn_sem, inc=1, device_id=place(me + 8), device_id_type=MESH)

        @pl.when(late)
        def _():
            pl.semaphore_wait(turn_sem, 1)
            for k in (2,):
                map_copy(own - 1, k).start()


    def add_low(both, low):
        return jnp.concatenate([both[:d], both[d:] + low], axis=0)

    def compose(j):
        gath[pos, j] = maps[4 * j + pos]
        for k in range(3):
            map_from(j, k).wait_recv()
        m = [gath[i, j] for i in range(4)]
        second = square(m[1][:d])
        third = square(m[2][:d])
        m01 = add_low(mm4(wide(m[0]), second, d), m[1][d:])
        m23 = add_low(mm4(wide(m[2]), square(m[3][:d]), d), m[3][d:])
        w01 = wide(m01)
        whole = add_low(mm4(w01, square(m23[:d]), d), m23[d:])
        total[j] = whole

        if direct:
            @pl.when(quad == 0)
            def _():
                x_copy(j, total.at[j, pl.ds(d, d)], 1).start()
                x_copy(j, total.at[j, pl.ds(d, d)], 2).start()

            @pl.when((quad == 1) | (quad == 2))
            def _():
                y_copy(j).start()

        m012 = add_low(mm4(w01, third, d), m[2][d:])
        for i, x in enumerate((m[0], m01, m012)):
            pre_sq[j, i] = square(x[:d])
            pre[j, i] = x[d:]

    def give(j, start):
        starts[j, 0] = start
        rows = wide(start)
        for i in range(3):
            starts[j, i + 1] = mm4(rows, pre_sq[j, i], d) + pre[j, i]
        for k in (2, 0, 1):
            back_copy(j, k).start()

    def pass_on(j, start, hop):
        x_out[j] = mm4(wide(start), square(total[j, :d]), d) + total[j, d:]
        x_copy(j, x_out.at[j], hop).start()

    for j in range(own):
        compose(j)

        @pl.when(quad == 0)
        def _():
            if not direct:
                x_copy(j, total.at[j, pl.ds(d, d)], 1).start()
            give(j, jnp.zeros((d, d), f32))

    for j in range(own):
        if direct:
            @pl.when(quad == 1)
            def _():
                x_copy(j, x_out.at[j], 1).wait_recv()
                pass_on(j, x_in[j], 2)
                give(j, x_in[j])

            @pl.when(quad >= 2)
            def _():
                y_copy(j).wait_recv()
                x_copy(j, x_out.at[j], 1).wait_recv()
                give(j, mm4(wide(x_in[j]), square(y_in[j, :d]), d) + y_in[j, d:])
        else:
            @pl.when(quad >= 1)
            def _():
                x_copy(j, x_out.at[j], 1).wait_recv()

                @pl.when(quad < quads - 1)
                def _():
                    pass_on(j, x_in[j], 1)

                give(j, x_in[j])

    gain = gain_ref[...]

    def readouts(pairs):
        boths = [nt(r_ref[h], square_t(state_t)) for h, state_t in pairs]
        outs = [both[:, :d] + both[:, d:] + lo_ref[h] for both, (h, _) in zip(boths, pairs)]
        scales = [lax.rsqrt(jnp.mean(out * out, axis=-1, keepdims=True) + eps_norm) for out in outs]
        spans = [pl.ds(pl.multiple_of(h * d, d), d) for h, _ in pairs]
        gates = [gate_ref[:, cols].astype(f32) for cols in spans]
        done = [
            (out * scale * gain * (g / (1.0 + jnp.exp(-g)))).astype(bf16)
            for out, scale, g in zip(outs, scales, gates)
        ]
        for cols, x in zip(spans, done):
            o_ref[:, cols] = x

    for j in range(own):
        for k in range(3):
            @pl.when(late | (j < own - 1) | (not direct) | (k not in (2,)))
            def _():
                map_copy(j, k).wait_send()

    for j in range(own):
        readouts([(4 * j + pos, starts[j, pos])])
        for k in range(3):
            back_copy(j, k).wait_recv()
        readouts([(4 * j + at, states[4 * j + at]) for at in places])

    for j in range(own):
        for k in range(3):
            back_copy(j, k).wait_send()
        if direct:
            @pl.when(quad == 0)
            def _():
                x_copy(j, total.at[j, pl.ds(d, d)], 1).wait_send()

            @pl.when(quad < 2)
            def _():
                x_copy(j, x_out.at[j], 2).wait_send()

            @pl.when((quad == 1) | (quad == 2))
            def _():
                y_copy(j).wait_send()
        else:
            @pl.when(quad < quads - 1)
            def _():
                x_copy(j, x_out.at[j], 1).wait_send()


def solution(mesh):
    inner = mesh.shape["inner"]
    count = inner * mesh.shape["outer"]
    assert count % 4 == 0

    def local(queries, keys, values, log_gate, out_gate, norm_gain):
        toks, width = queries.shape
        heads = log_gate.shape[1]
        d = width // heads
        own = heads // 4
        dma = pltpu.SemaphoreType.DMA
        return pl.pallas_call(
            lambda *refs: kernel(inner, count, *refs),
            out_shape=jax.ShapeDtypeStruct((toks, width), bf16),
            in_specs=[pl.BlockSpec(memory_space=pltpu.HBM)] * 6,
            out_specs=pl.BlockSpec(memory_space=pltpu.VMEM),
            scratch_shapes=[
                pltpu.VMEM((toks, 2, width), bf16),
                pltpu.VMEM((toks, 2, width), bf16),
                pltpu.VMEM((2 * toks, width), bf16),
                pltpu.VMEM((2 * toks, width), bf16),
                pltpu.VMEM((toks, width), bf16),
                pltpu.VMEM((heads, toks), f32),
                pltpu.VMEM((toks, width), bf16),
                pltpu.VMEM((1, d), f32),
                dma((2 * heads + 4,)),
                pltpu.VMEM((heads, 2 * d, d), f32),
                pltpu.VMEM((4, own, 2 * d, d), f32),
                pltpu.VMEM((own, 3, d, d), f32),
                pltpu.VMEM((own, 3, 2 * d, 2 * d), bf16),
                pltpu.VMEM((own, 2 * d, d), f32),
                pltpu.VMEM((heads, d, 2 * d), bf16),
                pltpu.VMEM((heads, d, d), f32),
                pltpu.VMEM((own, d, d), f32),
                pltpu.VMEM((own, 2 * d, d), f32),
                pltpu.VMEM((own, d, d), f32),
                pltpu.VMEM((own, 4, d, d), f32),
                pltpu.VMEM((heads, d, d), f32),
                dma((heads,)), dma((own, 4)), dma((own, 2)), dma((own,)),
                dma((own,)), dma((own,)), dma((own, 3)), dma((own, 3)),
                pltpu.SemaphoreType.REGULAR,
            ],
            compiler_params=pltpu.CompilerParams(
                collective_id=0, has_side_effects=True, vmem_limit_bytes=48 << 20
            ),
            name="delta_product",
        )(*[pltpu.with_memory_space_constraint(x, pltpu.HBM) for x in (keys, values, queries, log_gate.T, out_gate, norm_gain.reshape(1, d))])

    spec = P(("groups", "outer", "inner"), None)
    spec3 = P(("groups", "outer", "inner"), None, None)
    return jax.shard_map(
        local, mesh=mesh, in_specs=(spec, spec3, spec3, spec, spec, P()), out_specs=spec, check_vma=False
    )
```

```python
import jax
import jax.numpy as jnp
from jax import lax
from jax.experimental import pallas as pl
from jax.experimental.pallas import tpu as pltpu
from jax.sharding import PartitionSpec as P

eps_norm = 1e-06
f32 = jnp.float32
bf16 = jnp.bfloat16
MESH = pl.DeviceIdType.MESH
NT = (((1,), (1,)), ((), ()))
TN = (((0,), (0,)), ((), ()))


def mm(a, b):
    return jnp.dot(a, b, preferred_element_type=f32)


def split2(x):
    hi = x.astype(bf16)
    return hi, (x - hi.astype(f32)).astype(bf16)


def split3(x):
    hi, rest = x.astype(bf16), None
    rest = x - hi.astype(f32)
    mid = rest.astype(bf16)
    return hi, mid, (rest - mid.astype(f32)).astype(bf16)


def wide(x):
    return jnp.concatenate(split2(x), axis=1)


def square(x):
    row = jnp.concatenate(split2(x), axis=1)
    return jnp.concatenate([row, row], axis=0)


def mm4(a_wide, b_square, size):
    both = mm(a_wide, b_square)
    return both[:, :size] + both[:, size:]


def twice(x):
    return jnp.concatenate([x, x], axis=0)


def square_t(x):
    hi, lo = split2(x)
    return jnp.concatenate(
        [jnp.concatenate([hi, hi], axis=1), jnp.concatenate([lo, lo], axis=1)], axis=0
    )


def iotas(r, c):
    return (
        lax.broadcasted_iota(jnp.int32, (r, c), 0),
        lax.broadcasted_iota(jnp.int32, (r, c), 1),
    )


def nt(a, b):
    return lax.dot_general(a, b, NT, preferred_element_type=f32)


def kernel(inner, count, k_hbm, v_hbm, q_hbm, lg_hbm, gate_hbm, gain_hbm, o_ref,
           k_ref, v_ref, k_rows, v_rows, q_ref, lg_ref, gate_ref, gain_ref, in_sems, maps, gath, pre, pre_sq, total, r_ref, lo_ref, factor_ref, x_in, y_in, x_out, starts, states,
           map_send, map_recv, x_send, x_recv, y_send, y_recv, back_send, back_recv, turn_sem):
    toks, width = q_ref.shape
    steps = 2 * toks
    heads = lg_ref.shape[0]
    d = width // heads
    half = steps // 2
    own = heads // 4
    quads = count // 4
    direct = quads == 4

    me = lax.axis_index("outer") * inner + lax.axis_index("inner")
    pos = me % 4
    quad = me // 4
    places = [pos + 1 - 2 * (pos % 2), pos + 2 - 4 * (pos // 2), 3 - pos]

    def place(i):
        return {"outer": i // inner, "inner": i % inner}

    barrier = pltpu.get_barrier_semaphore()

    def greet(i):
        pl.semaphore_signal(barrier, inc=1, device_id=place(i), device_id_type=MESH)

    for at in places:
        greet(4 * quad + at)

    @pl.when(quad >= 1)
    def _():
        greet(me - 4)

    if direct:
        @pl.when(quad >= 2)
        def _():
            greet(me - 8)

    def greeted():
        hops = 2 if direct else 1

        for more in range(hops + 1):
            @pl.when((quad < quads - hops) if more == hops else (quad == quads - 1 - more))
            def _():
                pl.semaphore_wait(barrier, 3 + more)

    def remote(src, dst, send, recv, target):
        return pltpu.make_async_remote_copy(
            src_ref=src, dst_ref=dst, send_sem=send, recv_sem=recv,
            device_id=place(target), device_id_type=MESH,
        )

    def map_copy(j, k):
        h = 4 * j + places[k]
        return remote(maps.at[h], gath.at[pos, j], map_send.at[h], map_recv.at[j, pos], 4 * quad + places[k])

    def map_from(j, k):
        return remote(maps.at[0], gath.at[places[k], j], map_send.at[0], map_recv.at[j, places[k]],
                      4 * quad + places[k])

    def back_copy(j, k):
        return remote(starts.at[j, places[k]], states.at[4 * j + pos], back_send.at[j, k], back_recv.at[j, k],
                      4 * quad + places[k])

    def x_copy(j, src, hop):
        return remote(src, x_in.at[j], x_send.at[j, hop - 1], x_recv.at[j], me + 4 * hop)

    def y_copy(j):
        return remote(total.at[j], y_in.at[j], y_send.at[j], y_recv.at[j], me + 4)

    def fetch(h, which):
        src, dst = ((k_hbm, k_ref), (v_hbm, v_ref))[which]
        cols = pl.ds(h * d, d)
        return pltpu.make_async_copy(src.at[:, :, cols], dst.at[:, :, cols], in_sems.at[2 * h + which])

    others = [
        pltpu.make_async_copy(src, dst, in_sems.at[2 * heads + i])
        for i, (src, dst) in enumerate(
            ((lg_hbm, lg_ref), (q_hbm, q_ref), (gate_hbm, gate_ref), (gain_hbm, gain_ref))
        )
    ]
    others[0].start()
    for h in range(heads):
        fetch(h, 0).start()
        fetch(h, 1).start()
    for copy in others[1:]:
        copy.start()

    i_st, j_tk = iotas(steps, toks)
    tri_steps = (j_tk <= i_st // 2).astype(f32).astype(bf16)
    i_tk, j_tk2 = iotas(toks, toks)
    tri_toks = (j_tk2 <= i_tk).astype(f32).astype(bf16)
    others[0].wait()
    lgs = split3(lg_ref[...])
    c_col = sum(nt(tri_steps, p) for p in lgs)
    q_col = sum(nt(tri_toks, p) for p in lgs)
    c_row = sum(nt(p, tri_steps) for p in lgs)
    it, jt = iotas(toks, steps)
    visible = jt <= 2 * it + 1
    hi_, hj_ = iotas(half, half)
    eye = (hi_ == hj_).astype(f32)
    di, dj = iotas(d, d)
    levels = [2**i for i in range(1, half.bit_length() - 1)]
    corner = {
        b: ((hi_ // (2 * b) == hj_ // (2 * b)) & ((hi_ // b) % 2 == 1) & ((hj_ // b) % 2 == 0)).astype(f32).astype(bf16)
        for b in levels
    }
    below = hi_ > hj_
    close = hi_ // 2 == hj_ // 2
    eye_d = (di == dj).astype(f32)
    ones8 = jnp.ones((8, d), bf16)
    onesd = jnp.ones((d, d), bf16)

    nrow, solved = {}, {}
    keeps = {b: jnp.concatenate([corner[b]] * 2, axis=1) for b in levels}

    def solve(h):
        k_rows[:, h * d : (h + 1) * d] = k_ref[:, :, h * d : (h + 1) * d].reshape(steps, d)
        v_rows[:, h * d : (h + 1) * d] = v_ref[:, :, h * d : (h + 1) * d].reshape(steps, d)
        k = k_rows[:, h * d : (h + 1) * d]
        kf = k.astype(f32)
        sq = split2(kf * kf)
        yield
        n_c = lax.rsqrt(sum(mm(p, onesd) for p in sq) + eps_norm)
        n_r = lax.rsqrt(sum(nt(ones8, p) for p in sq) + eps_norm)[:1]
        nrow[h] = n_r
        c_h = jnp.broadcast_to(c_col[:, h : h + 1], (steps, d))
        row = c_row[h : h + 1, :]
        yield

        def coupled(i, j):
            at, to = slice(i * half, (i + 1) * half), slice(j * half, (j + 1) * half)
            gap = jnp.minimum(c_h[at] - row[:, to], 0.0)
            return jnp.exp(gap) * nt(k[at], k[to]) * (2.0 * n_r[:, to]) * n_c[at]

        diag = [jnp.where(below, coupled(i, i), 0.0) for i in range(2)]
        joint = coupled(1, 0)
        yield
        tri = [wide(x) for x in diag]
        invs = [eye - jnp.where(close, x, 0.0) for x in diag]
        wides = [wide(x) for x in invs]
        yield
        for b in levels:
            spans = [(i, i + b) for i in range(0, half, b)]

            def odd(x):
                return jnp.concatenate([x[p:q] for p, q in spans[1::2]], axis=0)

            def mixed(x, new):
                return jnp.concatenate(
                    [x[p:q] if n % 2 == 0 else new[(n // 2) * b : (n // 2 + 1) * b] for n, (p, q) in enumerate(spans)],
                    axis=0,
                )

            olds = invs if b < 8 else [odd(x) for x in invs]
            if b < 8:
                rows = wides
            elif b < 16:
                rows = [wide(x) for x in olds]
            else:
                rows = [odd(x) for x in wides]
            ts = [mm4(rows[i], twice(tri[i] * keeps[b]), half) for i in range(2)]
            yield
            ts = [wide(t) for t in ts]
            news = [olds[i] - mm4(ts[i], twice(wides[i]), half) for i in range(2)]
            yield
            if b < 8:
                invs = news
                wides = [wide(x) for x in invs]
            else:
                invs = [mixed(x, new) for x, new in zip(invs, news)]
                if b < 16:
                    wides = [wide(x) for x in invs]
                else:
                    wides = [mixed(x, wide(new)) for x, new in zip(wides, news)]
        first, second = wides
        t = mm4(second, square(joint), half)
        k = k_rows[:, h * d : (h + 1) * d].astype(f32)
        v = v_rows[:, h * d : (h + 1) * d]
        yield
        rhs = jnp.concatenate([v, wide(jnp.exp(c_h) * n_c * k)], axis=1)
        across = wide(-mm4(wide(t), twice(first), half))
        top = mm(first, twice(rhs[:half]))
        yield
        low = mm(jnp.concatenate([across, second], axis=1),
                 jnp.concatenate([twice(rhs[:half]), twice(rhs[half:])], axis=0))
        last = c_col[steps - 1 :, h : h + 1]
        tail = jnp.exp(c_h[steps - 1 :] - c_h) * (2.0 * n_c)
        t_hi, t_lo = split2(jnp.transpose(tail * k))
        yield
        x = jnp.concatenate([top, low], axis=0)
        x_hi, x_lo = split2(jnp.concatenate([x[:, :d], x[:, d : 2 * d] + x[:, 2 * d :]], axis=1))
        solved[h] = (x_hi, x_lo)
        yield
        ba = mm(t_hi, x_hi) + mm(t_lo, x_hi) + mm(t_hi, x_lo)
        yield
        ba = jnp.transpose(ba)
        maps[h] = jnp.concatenate([jnp.exp(last) * eye_d - ba[d:], ba[:d]], axis=0)

    def inside(h):
        k = k_rows[:, h * d : (h + 1) * d]
        x_hi, x_lo = solved[h]
        q = q_ref[:, h * d : (h + 1) * d]
        qc = q_col[:, h : h + 1]
        qgap = jnp.minimum(qc - c_row[h : h + 1, :], 0.0)
        pairs = jnp.where(visible, jnp.exp(qgap) * nt(q, k) * (2.0 * nrow[h]), 0.0)
        yield
        p_hi, p_lo = split2(pairs)
        px = mm(p_hi, x_hi) + mm(p_lo, x_hi) + mm(p_hi, x_lo)
        yield
        lo_ref[h] = px[:, :d]
        g = gate_ref[:, h * d : (h + 1) * d].astype(f32)
        factor_ref[h] = gain_ref[...] * (g / (1.0 + jnp.exp(-g)))
        r_ref[h] = wide(jnp.exp(qc) * q.astype(f32) - px[:, d:])

    def together(works, after=None, step=0):
        works = list(works)
        rounds = 0
        while works:
            works = [work for work in works if next(work, works) is not works]
            rounds += 1
            if after is not None and rounds == step:
                after()

    early = me < inner

    def send(j, mine, order=(2, 0, 1)):
        @pl.when(mine)
        def _():
            for k in order:
                map_copy(j, k).start()

    late = jnp.logical_not(early)
    for j in range(own):
        hs = range(4 * j, 4 * j + 4)
        for h in hs:
            fetch(h, 0).wait()
            fetch(h, 1).wait()
        together((solve(h) for h in hs), )
        if j == 0:
            greeted()
        send(j, early)
        if j < own - 1:
            send(j, late, (0, 1, 2))

    if direct:
        @pl.when(late)
        def _():
            for k in (0, 1):
                map_copy(own - 1, k).start()
    else:
        send(own - 1, late)
    for copy in others[1:]:
        copy.wait()
    for j in range(own):
        together(inside(h) for h in range(4 * j, 4 * j + 4))
    if direct:
        @pl.when(early)
        def _():
            for k in (2,):
                map_copy(own - 1, k).wait_send()
            pl.semaphore_signal(turn_sem, inc=1, device_id=place(me + 8), device_id_type=MESH)

        @pl.when(late)
        def _():
            pl.semaphore_wait(turn_sem, 1)
            for k in (2,):
                map_copy(own - 1, k).start()


    def add_low(both, low):
        return jnp.concatenate([both[:d], both[d:] + low], axis=0)

    def compose(j):
        gath[pos, j] = maps[4 * j + pos]
        for k in range(3):
            map_from(j, k).wait_recv()
        m = [gath[i, j] for i in range(4)]
        second = square(m[1][:d])
        third = square(m[2][:d])
        m01 = add_low(mm4(wide(m[0]), second, d), m[1][d:])
        m23 = add_low(mm4(wide(m[2]), square(m[3][:d]), d), m[3][d:])
        w01 = wide(m01)
        whole = add_low(mm4(w01, square(m23[:d]), d), m23[d:])
        total[j] = whole

        if direct:
            @pl.when(quad == 0)
            def _():
                x_copy(j, total.at[j, pl.ds(d, d)], 1).start()
                x_copy(j, total.at[j, pl.ds(d, d)], 2).start()

            @pl.when((quad == 1) | (quad == 2))
            def _():
                y_copy(j).start()

        m012 = add_low(mm4(w01, third, d), m[2][d:])
        for i, x in enumerate((m[0], m01, m012)):
            pre_sq[j, i] = square(x[:d])
            pre[j, i] = x[d:]

    def give(j, start):
        starts[j, 0] = start
        rows = wide(start)
        for i in range(3):
            starts[j, i + 1] = mm4(rows, pre_sq[j, i], d) + pre[j, i]
        for k in (2, 0, 1):
            back_copy(j, k).start()

    def pass_on(j, start, hop):
        x_out[j] = mm4(wide(start), square(total[j, :d]), d) + total[j, d:]
        x_copy(j, x_out.at[j], hop).start()

    for j in range(own):
        compose(j)

        @pl.when(quad == 0)
        def _():
            if not direct:
                x_copy(j, total.at[j, pl.ds(d, d)], 1).start()
            give(j, jnp.zeros((d, d), f32))

    for j in range(own):
        if direct:
            @pl.when(quad == 1)
            def _():
                x_copy(j, x_out.at[j], 1).wait_recv()
                pass_on(j, x_in[j], 2)
                give(j, x_in[j])

            @pl.when(quad >= 2)
            def _():
                y_copy(j).wait_recv()
                x_copy(j, x_out.at[j], 1).wait_recv()
                give(j, mm4(wide(x_in[j]), square(y_in[j, :d]), d) + y_in[j, d:])
        else:
            @pl.when(quad >= 1)
            def _():
                x_copy(j, x_out.at[j], 1).wait_recv()

                @pl.when(quad < quads - 1)
                def _():
                    pass_on(j, x_in[j], 1)

                give(j, x_in[j])


    def readouts(pairs):
        boths = [nt(r_ref[h], square_t(state_t)) for h, state_t in pairs]
        outs = [both[:, :d] + both[:, d:] + lo_ref[h] for both, (h, _) in zip(boths, pairs)]
        scales = [lax.rsqrt(jnp.mean(out * out, axis=-1, keepdims=True) + eps_norm) for out in outs]
        spans = [pl.ds(pl.multiple_of(h * d, d), d) for h, _ in pairs]
        done = [(out * scale * factor_ref[h]).astype(bf16) for out, scale, (h, _) in zip(outs, scales, pairs)]
        for cols, x in zip(spans, done):
            o_ref[:, cols] = x

    for j in range(own):
        for k in range(3):
            @pl.when(late | (j < own - 1) | (not direct) | (k not in (2,)))
            def _():
                map_copy(j, k).wait_send()

    for j in range(own):
        readouts([(4 * j + pos, starts[j, pos])])
        for k in range(3):
            back_copy(j, k).wait_recv()
        readouts([(4 * j + at, states[4 * j + at]) for at in places])

    for j in range(own):
        for k in range(3):
            back_copy(j, k).wait_send()
        if direct:
            @pl.when(quad == 0)
            def _():
                x_copy(j, total.at[j, pl.ds(d, d)], 1).wait_send()

            @pl.when(quad < 2)
            def _():
                x_copy(j, x_out.at[j], 2).wait_send()

            @pl.when((quad == 1) | (quad == 2))
            def _():
                y_copy(j).wait_send()
        else:
            @pl.when(quad < quads - 1)
            def _():
                x_copy(j, x_out.at[j], 1).wait_send()


def solution(mesh):
    inner = mesh.shape["inner"]
    count = inner * mesh.shape["outer"]
    assert count % 4 == 0

    def local(queries, keys, values, log_gate, out_gate, norm_gain):
        toks, width = queries.shape
        heads = log_gate.shape[1]
        d = width // heads
        own = heads // 4
        dma = pltpu.SemaphoreType.DMA
        return pl.pallas_call(
            lambda *refs: kernel(inner, count, *refs),
            out_shape=jax.ShapeDtypeStruct((toks, width), bf16),
            in_specs=[pl.BlockSpec(memory_space=pltpu.HBM)] * 6,
            out_specs=pl.BlockSpec(memory_space=pltpu.VMEM),
            scratch_shapes=[
                pltpu.VMEM((toks, 2, width), bf16),
                pltpu.VMEM((toks, 2, width), bf16),
                pltpu.VMEM((2 * toks, width), bf16),
                pltpu.VMEM((2 * toks, width), bf16),
                pltpu.VMEM((toks, width), bf16),
                pltpu.VMEM((heads, toks), f32),
                pltpu.VMEM((toks, width), bf16),
                pltpu.VMEM((1, d), f32),
                dma((2 * heads + 4,)),
                pltpu.VMEM((heads, 2 * d, d), f32),
                pltpu.VMEM((4, own, 2 * d, d), f32),
                pltpu.VMEM((own, 3, d, d), f32),
                pltpu.VMEM((own, 3, 2 * d, 2 * d), bf16),
                pltpu.VMEM((own, 2 * d, d), f32),
                pltpu.VMEM((heads, d, 2 * d), bf16),
                pltpu.VMEM((heads, d, d), f32),
                pltpu.VMEM((heads, d, d), f32),
                pltpu.VMEM((own, d, d), f32),
                pltpu.VMEM((own, 2 * d, d), f32),
                pltpu.VMEM((own, d, d), f32),
                pltpu.VMEM((own, 4, d, d), f32),
                pltpu.VMEM((heads, d, d), f32),
                dma((heads,)), dma((own, 4)), dma((own, 2)), dma((own,)),
                dma((own,)), dma((own,)), dma((own, 3)), dma((own, 3)),
                pltpu.SemaphoreType.REGULAR,
            ],
            compiler_params=pltpu.CompilerParams(
                collective_id=0, has_side_effects=True, vmem_limit_bytes=48 << 20
            ),
            name="delta_product",
        )(*[pltpu.with_memory_space_constraint(x, pltpu.HBM) for x in (keys, values, queries, log_gate.T, out_gate, norm_gain.reshape(1, d))])

    spec = P(("groups", "outer", "inner"), None)
    spec3 = P(("groups", "outer", "inner"), None, None)
    return jax.shard_map(
        local, mesh=mesh, in_specs=(spec, spec3, spec3, spec, spec, P()), out_specs=spec, check_vma=False
    )
```
